32 devices in a mesh: dp: 16 (over z, x, core), tp: 2 (over y).
Axes of the slice: x: 2, y: 2, z: 4, core: 2. Of those that a mesh axis runs over, the one named last changes fastest.
Arguments:
- hidden_in: bfloat16 [28672, 1024], P('dp', 'tp'), may hold values from -6 to 6
- encoder_states: bfloat16 [64, 1500, 1024], P('dp'), may hold values from -6 to 6
- positions: int32 [64, 448], P('dp'), may hold values from 0 to 447, each once within a row
- self_qkv: bfloat16 [1024, 3, 1024], P('dp', None, 'tp'), may hold values from -0.1875 to 0.1875
- self_out: bfloat16 [1024, 1024], P('tp', 'dp'), may hold values from -1 to 1
- cross_query: bfloat16 [1024, 1024], P('dp', 'tp'), may hold values from -0.1875 to 0.1875
- cross_kv: bfloat16 [1024, 2, 1024], P('dp', None, 'tp'), may hold values from -0.1875 to 0.1875
- cross_out: bfloat16 [1024, 1024], P('tp', 'dp'), may hold values from -1.5 to 1.5
- up_weight: bfloat16 [1024, 4096], P('dp', 'tp'), may hold values from -0.1875 to 0.1875
- down_weight: bfloat16 [4096, 1024], P('tp', 'dp'), may hold values from -0.09375 to 0.09375
- norm_gains: float32 [3, 1024], P(None, 'tp'), may hold values from 0.5 to 1.5
- bias_rows: float32 [10, 1024], P(None, 'tp'), may hold values from -1.25 to 1.25
- up_bias: float32 [4096], P('tp'), may hold values from -1.25 to 1.25
- out_grad: bfloat16 [28672, 1024], P('dp', 'tp'), may hold values from -6 to 6
Outputs:
- output: bfloat16 [28672, 1024], P('dp', 'tp')
- hidden_grad: float32 [28672, 1024], P('dp', 'tp')
- encoder_grad: float32 [64, 1500, 1024], P('dp', None, 'tp')
- grad_self_qkv: float32 [1024, 3, 1024], P('dp', None, 'tp')
- grad_self_out: float32 [1024, 1024], P('tp', 'dp')
- grad_cross_query: float32 [1024, 1024], P('dp', 'tp')
- grad_cross_kv: float32 [1024, 2, 1024], P('dp', None, 'tp')
- grad_cross_out: float32 [1024, 1024], P('tp', 'dp')
- grad_up_weight: float32 [1024, 4096], P('dp', 'tp')
- grad_down_weight: float32 [4096, 1024], P('tp', 'dp')
- grad_norm_gains: float32 [3, 1024], P(None, 'tp')
- grad_bias_rows: float32 [10, 1024], P(None, 'tp')
- grad_up_bias: float32 [4096], P('tp')
The draws below stay inside these ranges and needn't reach their ends.
Inputs may be any that keep to these rules, and one draw needn't show every extreme that they name: `positions`: each row lists every position 0 to 447 once.
All inputs are finite; a program needn't handle non-finite values.
Results may differ from the reference program's by a relative error of at most 0.02.
Values may be sent and summed in bfloat16 or wider, within the bound.
No kernel may reach another device: no remote copies, remote signals or barrier semaphores. Data moves between devices by JAX's collectives and lax.ppermute only.
A program may use at most 512 MiB of HBM per device.

```python
import jax
import jax.numpy as jnp
from jax import lax

D = 1024
HEADS = 16
FF = 4096
FRAMES = 1500
LEN = 448
HEAD_DIM = 64
SEQS = 64
TOKENS = 28672


def block_scale(own_key, extent, cuts, low, largest):
    level, own = 1.0, jax.random.fold_in(own_key, 6)
    for axis_at, parts in cuts:
        steps = jnp.exp(jax.random.uniform(jax.random.fold_in(own, axis_at), (parts,), jnp.float32, low / len(cuts), largest / len(cuts)))
        level = level * jnp.repeat(steps, extent[axis_at] // parts).reshape([-1 if axis == axis_at else 1 for axis in range(len(extent))])
    return level


def bell_draw(rng, dims, deviation, bound, cuts=(), dtype=jnp.bfloat16):
    loudness = block_scale(rng, dims, cuts, -0.22, 0.18) if cuts else 1.0
    values = jax.random.normal(rng, dims, jnp.float32) * deviation * loudness
    return jnp.minimum(jnp.maximum(values, -bound), bound).astype(dtype)


def setup_inputs(seed: int = 0) -> dict:
    seeds = jax.random.split(jax.random.key(seed), 15)
    return {
        "hidden_in": bell_draw(seeds[0], (TOKENS, D), 1.0, 6.0, ((0, 16), (1, 2))),
        "encoder_states": bell_draw(seeds[1], (SEQS, FRAMES, D), 1.0, 6.0, ((0, 16),)),
        "positions": jax.vmap(lambda own: jax.random.permutation(own, LEN))(jax.random.split(seeds[2], SEQS)).reshape((SEQS, LEN)).astype(jnp.int32),
        "self_qkv": bell_draw(seeds[3], (D, 3, D), D ** -0.5, 0.1875, ((0, 16), (2, 2))),
        "self_out": bell_draw(seeds[4], (D, D), (D // 32) ** -0.5, 1.0, ((0, 2), (1, 16))),
        "cross_query": bell_draw(seeds[5], (D, D), D ** -0.5, 0.1875, ((0, 16), (1, 2))),
        "cross_kv": bell_draw(seeds[6], (D, 2, D), D ** -0.5, 0.1875, ((0, 16), (2, 2))),
        "cross_out": bell_draw(seeds[7], (D, D), (D // 64) ** -0.5, 1.5, ((0, 2), (1, 16))),
        "up_weight": bell_draw(seeds[8], (D, FF), D ** -0.5, 0.1875, ((0, 16), (1, 2))),
        "down_weight": bell_draw(seeds[9], (FF, D), FF ** -0.5, 0.09375, ((0, 2), (1, 16))),
        "norm_gains": jnp.clip(1.0 + 0.1 * jax.random.normal(seeds[10], (3, D), jnp.float32), 0.5, 1.5),
        "bias_rows": bell_draw(seeds[11], (10, D), 0.2, 1.25, ((1, 2),), jnp.float32),
        "up_bias": bell_draw(seeds[12], (FF,), 0.2, 1.25, ((0, 2),), jnp.float32),
        "out_grad": bell_draw(seeds[13], (TOKENS, D), 1.0, 6.0, ((0, 16), (1, 2))),
    }


HIGH = lax.Precision.HIGHEST
EPSILON = 1e-05
NEGATIVE = -1e+30

@jax.custom_vjp
def low(v):
    return lax.optimization_barrier(v.astype(jnp.bfloat16)).astype(jnp.float32)

@jax.custom_vjp
def low_back(v):
    return v

def low_keep(v):
    return (low(v), None)

def low_pass(kept, grad):
    return (grad,)

def back_keep(v):
    return (v, None)

def back_low(kept, grad):
    return (low(grad),)
low.defvjp(low_keep, low_pass)
low_back.defvjp(back_keep, back_low)

def rounded_both(value):
    return low(low_back(value))

def layer_norm(values, gain, shift):
    row_mean = lax.optimization_barrier(jnp.mean(values, axis=-1, keepdims=True))
    variance = lax.optimization_barrier(jnp.mean(values * values, axis=-1, keepdims=True)) - row_mean * row_mean
    return (values - row_mean) * lax.rsqrt(variance + EPSILON) * gain + shift

def heads_of(matrix):
    return matrix.reshape(matrix.shape[0], HEADS, HEAD_DIM)

def attention(query, key_rows, value_rows, visible):
    scores = jnp.einsum('qhe,khe->hqk', heads_of(query), heads_of(key_rows), precision=HIGH) * HEAD_DIM ** (-0.5)
    scores = low_back(scores)
    if visible is not None:
        scores = jnp.where(visible[None], scores, NEGATIVE)
    row_max = lax.optimization_barrier(jnp.max(scores, axis=-1, keepdims=True))
    weights = jnp.exp(scores - row_max)
    weights = low(weights / lax.optimization_barrier(jnp.sum(weights, axis=-1, keepdims=True)))
    mixed = jnp.einsum('hqk,khe->qhe', weights, heads_of(value_rows), precision=HIGH)
    return mixed.reshape(query.shape[0], D)

def one_sequence(params, hidden, frames, order):
    self_qkv, self_out, cross_query, cross_kv, cross_out, up_weight, down_weight, norm_gains, bias_rows, up_bias = params
    visible = order[None, :] <= order[:, None]
    normed = low(layer_norm(hidden, norm_gains[0], bias_rows[0]))
    triple = jnp.einsum('td,dcf->tcf', normed, self_qkv, precision=HIGH)
    query = rounded_both(triple[:, 0] + bias_rows[3])
    key_rows = rounded_both(triple[:, 1])
    value_rows = rounded_both(triple[:, 2] + bias_rows[4])
    mixed = rounded_both(attention(query, key_rows, value_rows, visible))
    first = hidden + low_back(jnp.dot(mixed, self_out, precision=HIGH) + bias_rows[5])
    cross_in = low(layer_norm(first, norm_gains[1], bias_rows[1]))
    cross_q = rounded_both(jnp.dot(cross_in, cross_query, precision=HIGH) + bias_rows[6])
    paired = jnp.einsum('fd,dcg->fcg', frames, cross_kv, precision=HIGH)
    cross_k = rounded_both(paired[:, 0])
    cross_v = rounded_both(paired[:, 1] + bias_rows[7])
    cross_mixed = rounded_both(attention(cross_q, cross_k, cross_v, None))
    second = first + low_back(jnp.dot(cross_mixed, cross_out, precision=HIGH) + bias_rows[8])
    mlp_in = low(layer_norm(second, norm_gains[2], bias_rows[2]))
    before = low_back(jnp.dot(mlp_in, up_weight, precision=HIGH) + up_bias)
    activated = low(jax.nn.gelu(before, approximate=False))
    return second + low_back(jnp.dot(activated, down_weight, precision=HIGH) + bias_rows[9])

def reference(hidden_in, encoder_states, positions, self_qkv, self_out, cross_query, cross_kv, cross_out, up_weight, down_weight, norm_gains, bias_rows, up_bias, out_grad):
    params = (self_qkv.astype(jnp.float32), self_out.astype(jnp.float32), cross_query.astype(jnp.float32), cross_kv.astype(jnp.float32), cross_out.astype(jnp.float32), up_weight.astype(jnp.float32), down_weight.astype(jnp.float32), norm_gains.astype(jnp.float32), bias_rows.astype(jnp.float32), up_bias.astype(jnp.float32))
    hidden = hidden_in.astype(jnp.float32).reshape(-1, LEN, D)
    frames = encoder_states.astype(jnp.float32)

    def all_sequences(weights_now, hidden_now, frames_now):

        def per_sequence(carried, pieces):
            return (carried, jax.checkpoint(one_sequence)(weights_now, pieces[0], pieces[1], pieces[2]))
        _, results = lax.scan(per_sequence, jnp.zeros((), jnp.float32), (hidden_now, frames_now, positions))
        return results
    result, pullback = jax.vjp(all_sequences, params, hidden, frames)
    weight_grads, hidden_grad, encoder_grad = pullback(out_grad.astype(jnp.float32).reshape(-1, LEN, D))
    return (result.reshape(-1, D).astype(jnp.bfloat16), hidden_grad.reshape(-1, D), encoder_grad, weight_grads[0], weight_grads[1], weight_grads[2], weight_grads[3], weight_grads[4], weight_grads[5], weight_grads[6], weight_grads[7], weight_grads[8], weight_grads[9])
```

```python
import functools
import math

import jax
import jax.numpy as jnp
from jax import lax
from jax.experimental import pallas as pl
from jax.experimental.pallas import tpu as pltpu
from jax.sharding import PartitionSpec as P

D = 1024
LEN = 448
SEQ_MB = 1
MICRO = 4
HEAD_DIM = 64
BF = jnp.bfloat16
F32 = jnp.float32
LANES = 128


EPSILON = 1e-05
NEGATIVE = -1e30

QKV, CKV, OUT, CQ, CO = 0, 3, 5, 6, 7
VMEM_BYTES = 58 << 20


def nn(a, b):
    return jnp.dot(a, b, preferred_element_type=F32)


def nt(a, b):
    return lax.dot_general(a, b, (((1,), (1,)), ((), ())), preferred_element_type=F32)


def tn(a, b):
    return lax.dot_general(a, b, (((0,), (0,)), ((), ())), preferred_element_type=F32)


def compiler_params(axes):
    return pltpu.CompilerParams(
        dimension_semantics=("arbitrary",) * axes, vmem_limit_bytes=VMEM_BYTES
    )


def cost(flops, *arrays):
    return pl.CostEstimate(flops=1, bytes_accessed=1, transcendentals=0)


def struct(shape, dtype):
    return jax.ShapeDtypeStruct(shape, dtype)


def weight(ref):
    block = ref[0, :, 0]
    return block.reshape(block.shape[0] * block.shape[1], block.shape[2])


def weight_spec(gathered, index):
    _, shards, _, rows, width = gathered.shape

    def index_map(*grid):
        column, block = index(*grid)
        return (column, 0, block, 0, 0)

    return pl.BlockSpec((1, shards, 1, rows, width), index_map)


def whole(array):
    return pl.BlockSpec(array.shape, lambda *grid: (0,) * len(array.shape))


def row_loop(rows, body):
    step = 128 if rows % 128 == 0 else 64

    def run(at, carried):
        body(pl.ds(pl.multiple_of(at * step, step), step))
        return carried

    lax.fori_loop(0, rows // step, run, 0)


def norm_stats(values):
    row_mean = jnp.mean(values, axis=1, keepdims=True)
    square = jnp.mean(values * values, axis=1, keepdims=True)
    return row_mean, lax.rsqrt(square - row_mean * row_mean + EPSILON)


def write_norm(source_ref, normed_ref, gain, shift):
    def body(rows):
        values = source_ref[rows, :].astype(F32)
        row_mean, inverse = norm_stats(values)
        normed_ref[rows, :] = ((values - row_mean) * inverse * gain + shift).astype(BF)

    row_loop(source_ref.shape[0], body)


def write_norm_back(grad_ref, source_ref, gain, sums_ref, finish):
    sums_ref[...] = jnp.zeros_like(sums_ref)

    def body(rows):
        incoming = grad_ref[rows, :]
        values = source_ref[rows, :].astype(F32)
        row_mean, inverse = norm_stats(values)
        unit = (values - row_mean) * inverse
        scaled = incoming * gain
        back = inverse * (
            scaled
            - jnp.mean(scaled, axis=1, keepdims=True)
            - unit * jnp.mean(scaled * unit, axis=1, keepdims=True)
        )
        low = finish(rows, back)
        sums_ref[0:1, :] += jnp.sum(incoming * unit, axis=0, keepdims=True)
        sums_ref[1:2, :] += jnp.sum(incoming, axis=0, keepdims=True)
        sums_ref[2:3, :] += jnp.sum(low.astype(F32), axis=0, keepdims=True)

    row_loop(grad_ref.shape[0], body)


def qkv_kernel(hidden_ref, vec_ref, w_ref, bias_ref, out_ref, normed_ref):
    @pl.when((pl.program_id(0) == 0) & (pl.program_id(1) == 0))
    def _():
        write_norm(hidden_ref, normed_ref, vec_ref[0:1, :], vec_ref[3:4, :])

    out_ref[0, 0] = (nn(normed_ref[...], weight(w_ref)) + bias_ref[0, 0]).astype(BF)


def project_qkv(hidden, vec, gathered, bias):
    columns, width = gathered.shape[0], gathered.shape[-1]
    tokens = hidden.shape[0]
    return pl.pallas_call(
        qkv_kernel,
        grid=(columns, 3),
        in_specs=[
            whole(hidden),
            whole(vec),
            weight_spec(gathered, lambda y, c: (y, QKV + c)),
            pl.BlockSpec((1, 1, 1, width), lambda y, c: (y, c, 0, 0)),
        ],
        out_specs=[
            pl.BlockSpec((1, 1, tokens, width), lambda y, c: (y, c, 0, 0)),
            whole(hidden),
        ],
        out_shape=[struct((columns, 3, tokens, width), BF), struct(hidden.shape, BF)],
        compiler_params=compiler_params(2),
        cost_estimate=cost(2 * tokens * D * 3 * columns * width, hidden, hidden),
        name="project_qkv",
    )(hidden, vec, gathered, bias)


def head_row(head, value):
    lane = lax.broadcasted_iota(jnp.int32, (1, LANES), 1)
    inside = (lane >= head * HEAD_DIM) & (lane < (head + 1) * HEAD_DIM)
    return jnp.where(inside, value, 0.0).astype(BF)


def attend(query, key_rows, value_rows, visible, mixed_ref, probs_ref):
    parts = []
    for head in range(LANES // HEAD_DIM):
        scores = nt(key_rows, query * head_row(head, HEAD_DIM**-0.5))
        if visible is not None:
            scores = jnp.where(visible, scores, NEGATIVE)
        weights = jnp.exp(scores - jnp.max(scores, axis=0, keepdims=True))
        inverse = 1.0 / jnp.sum(weights, axis=0, keepdims=True)
        probs = (weights * inverse).astype(BF)
        probs_ref[0, 0, 0, head] = probs
        part = tn(value_rows, probs)
        parts.append(part[head * HEAD_DIM : (head + 1) * HEAD_DIM])
    mixed_ref[0] = jnp.concatenate(parts, axis=0).T.astype(BF)


def attend_back(query, key_rows, value_rows, mixed, grad_mixed, probs_ref):
    grad_f = grad_mixed.astype(F32)
    product = (grad_f * mixed.astype(F32)).T
    parts, grad_key, grad_value = [], 0.0, 0.0
    for head in range(LANES // HEAD_DIM):
        span = slice(head * HEAD_DIM, (head + 1) * HEAD_DIM)
        inner = jnp.sum(product[span], axis=0, keepdims=True)
        own_grad = grad_mixed * head_row(head, 1.0)
        probs = probs_ref[0, 0, 0, head]
        grad_weights = nt(value_rows, own_grad)
        grad_scores = (probs.astype(F32) * (grad_weights - inner)).astype(BF)
        grad_key = grad_key + nn(grad_scores, query * head_row(head, HEAD_DIM**-0.5))
        grad_value = grad_value + nn(probs, own_grad)
        parts.append(tn(key_rows, grad_scores)[span])
    grad_query = jnp.concatenate(parts, axis=0).T * HEAD_DIM**-0.5
    return grad_query.astype(BF), grad_key.astype(BF), grad_value.astype(BF)


def self_kernel(q_ref, k_ref, v_ref, row_ref, column_ref, mixed_ref, probs_ref):
    visible = column_ref[0] <= row_ref[0]
    attend(q_ref[0, 0], k_ref[0, 0], v_ref[0, 0], visible, mixed_ref, probs_ref)


def attend_self(qkv, order_row, order_column):
    columns, _, tokens, width = qkv.shape
    seqs, pairs = order_row.shape[0], width // LANES

    def part(c):
        return pl.BlockSpec((1, 1, LEN, LANES), lambda y, p, s: (y, c, s, p))

    return pl.pallas_call(
        self_kernel,
        grid=(columns, pairs, seqs),
        in_specs=[
            part(0),
            part(1),
            part(2),
            pl.BlockSpec((1, 1, LEN), lambda y, p, s: (s, 0, 0)),
            pl.BlockSpec((1, LEN, 1), lambda y, p, s: (s, 0, 0)),
        ],
        out_specs=[
            pl.BlockSpec((1, LEN, LANES), lambda y, p, s: (y, s, p)),
            pl.BlockSpec((1, 1, 1, 2, LEN, LEN), lambda y, p, s: (y, p, s, 0, 0, 0)),
        ],
        out_shape=[
            struct((columns, tokens, width), BF),
            struct((columns, pairs, seqs, 2, LEN, LEN), BF),
        ],
        compiler_params=compiler_params(3),
        cost_estimate=cost(16 * columns * pairs * seqs * LEN * LEN * LANES, qkv),
        name="attend_self",
    )(qkv, qkv, qkv, order_row, order_column)


def out_kernel(mixed_ref, hidden_ref, vec_ref, wo_ref, wq_ref, bias_ref, first_ref, normed_ref, query_ref):
    step, columns = pl.program_id(0), pl.num_programs(0) // 2

    @pl.when(step == 0)
    def _():
        first_ref[...] = hidden_ref[...].astype(F32) + vec_ref[8:9, :]

    @pl.when(step < columns)
    def _():
        first_ref[...] += nt(mixed_ref[0], weight(wo_ref))

    @pl.when(step == columns - 1)
    def _():
        write_norm(first_ref, normed_ref, vec_ref[1:2, :], vec_ref[4:5, :])

    @pl.when(step >= columns)
    def _():
        query_ref[0] = (nn(normed_ref[...], weight(wq_ref)) + bias_ref[0]).astype(BF)


def project_out(mixed, hidden, vec, gathered, bias):
    columns, tokens, width = mixed.shape

    def early(i):
        return jnp.minimum(i, columns - 1)

    def late(i):
        return jnp.maximum(i - columns, 0)

    return pl.pallas_call(
        out_kernel,
        grid=(2 * columns,),
        in_specs=[
            pl.BlockSpec((1, tokens, width), lambda i: (early(i), 0, 0)),
            whole(hidden),
            whole(vec),
            weight_spec(gathered, lambda i: (early(i), OUT)),
            weight_spec(gathered, lambda i: (late(i), CQ)),
            pl.BlockSpec((1, 1, width), lambda i: (late(i), 0, 0)),
        ],
        out_specs=[
            whole(hidden),
            whole(hidden),
            pl.BlockSpec((1, tokens, width), lambda i: (late(i), 0, 0)),
        ],
        out_shape=[
            struct(hidden.shape, F32),
            struct(hidden.shape, BF),
            struct((columns, tokens, width), BF),
        ],
        compiler_params=compiler_params(1),
        cost_estimate=cost(4 * tokens * D * columns * width, hidden, hidden, mixed),
        name="project_out",
    )(mixed, hidden, vec, gathered, gathered, bias)


def pair_kernel(own_ref, frames_ref, w_ref, bias_ref, out_ref):
    out_ref[0, 0, 0] = (nn(frames_ref[0], weight(w_ref)) + bias_ref[0, 0]).astype(BF)


def project_pair(own, frames, gathered, bias, seqs):
    columns, width = gathered.shape[0], gathered.shape[-1]
    length = frames.shape[1]
    out = struct((columns, 2, seqs, length, width), BF)
    return pl.pallas_call(
        pair_kernel,
        grid_spec=pltpu.PrefetchScalarGridSpec(
            num_scalar_prefetch=1,
            grid=(seqs, columns, 2),
            in_specs=[
                pl.BlockSpec((1, length, D), lambda s, y, c, own: (s, 0, 0)),
                weight_spec(gathered, lambda s, y, c, own: (y, CKV + c)),
                pl.BlockSpec((1, 1, 1, width), lambda s, y, c, own: (y, c, 0, 0)),
            ],
            out_specs=pl.BlockSpec((1, 1, 1, length, width), lambda s, y, c, own: (y, c, s, 0, 0)),
        ),
        out_shape=out,
        compiler_params=compiler_params(3),
        cost_estimate=cost(4 * seqs * length * D * columns * width, out, out),
        name="project_pair",
    )(own, frames, gathered, bias)


def cross_kernel(q_ref, kv_ref, mixed_ref, probs_ref):
    attend(q_ref[0], kv_ref[0, 0, 0], kv_ref[0, 1, 0], None, mixed_ref, probs_ref)


def attend_cross(query, pair):
    columns, tokens, width = query.shape
    seqs, length, pairs = pair.shape[2], pair.shape[3], width // LANES
    return pl.pallas_call(
        cross_kernel,
        grid=(columns, pairs, seqs),
        in_specs=[
            pl.BlockSpec((1, LEN, LANES), lambda y, p, s: (y, s, p)),
            pl.BlockSpec((1, 2, 1, length, LANES), lambda y, p, s: (y, 0, s, 0, p)),
        ],
        out_specs=[
            pl.BlockSpec((1, LEN, LANES), lambda y, p, s: (y, s, p)),
            pl.BlockSpec((1, 1, 1, 2, length, LEN), lambda y, p, s: (y, p, s, 0, 0, 0)),
        ],
        out_shape=[
            struct((columns, tokens, width), BF),
            struct((columns, pairs, seqs, 2, length, LEN), BF),
        ],
        compiler_params=compiler_params(3),
        cost_estimate=cost(16 * columns * pairs * seqs * LEN * length * LANES, pair),
        name="attend_cross",
    )(query, pair)


def erf(value):
    x = jnp.clip(value, -3.832506856900711, 3.832506856900711)
    square = x * x
    top = jnp.full_like(x, 0.00022905065861350646)
    for coefficient in (0.0034082910107109506, 0.050955695062380861, 0.18520832239976145, 1.128379143519084):
        top = top * square + coefficient
    bottom = jnp.full_like(x, -1.1791602954361697e-7)
    for coefficient in (
        0.000023547966471313185,
        0.0010179625278914885,
        0.014070470171167667,
        0.11098505178285362,
        0.49746925110067538,
        1.0,
    ):
        bottom = bottom * square + coefficient
    return x * top / bottom


def halves_of(value, own):
    width = value.shape[1] // 2
    low, high = value[:, :width], value[:, width:]
    return jnp.where(own == 0, high, low), jnp.where(own == 0, low, high)


def mlp_kernel(
    own_ref, mixed_ref, first_ref, vec_ref, wo_ref, wu_ref, wd_ref, bias_ref,
    second_ref, normed_ref, act_ref, slope_ref, send_ref, keep_ref, total_ref,
):
    step, columns = pl.program_id(0), 2

    @pl.when(step == 0)
    def _():
        second_ref[...] = first_ref[...] + vec_ref[11:12, :]

    @pl.when(step < columns)
    def _():
        second_ref[...] += nt(mixed_ref[0], weight(wo_ref))

    @pl.when(step == columns - 1)
    def _():
        write_norm(second_ref, normed_ref, vec_ref[2:3, :], vec_ref[5:6, :])
        total_ref[...] = second_ref[...] + vec_ref[12:13, :]

    @pl.when(step >= columns)
    def _():
        before = nn(normed_ref[...], weight(wu_ref)) + bias_ref[0, 0]
        cdf = 0.5 + 0.5 * erf(before * (0.5**0.5))
        density = jnp.exp(-0.5 * before * before) * (1.0 / math.sqrt(2.0 * math.pi))
        act = (before * cdf).astype(BF)
        act_ref[0, 0] = act
        slope_ref[0, 0] = (cdf + before * density).astype(BF)
        total_ref[...] += nt(act, weight(wd_ref))

    @pl.when(step == pl.num_programs(0) - 1)
    def _():
        send, keep = halves_of(total_ref[...], own_ref[0])
        send_ref[...] = send.astype(BF)
        keep_ref[...] = keep.astype(BF)


def mlp_forward(own, mixed, first, vec, gathered, gathered_mlp, bias):
    columns, tokens, width = mixed.shape
    blocks = gathered_mlp.shape[2] // 2

    def early(i):
        return jnp.minimum(i, columns - 1)

    def late(i):
        rest = jnp.maximum(i - columns, 0)
        return rest // blocks, rest % blocks

    units = struct((columns, blocks, tokens, width), BF)
    half = struct((tokens, width), BF)
    unit_spec = pl.BlockSpec((1, 1, tokens, width), lambda i, own: (*late(i), 0, 0))
    return pl.pallas_call(
        mlp_kernel,
        grid_spec=pltpu.PrefetchScalarGridSpec(
            num_scalar_prefetch=1,
            grid=(columns + columns * blocks,),
            in_specs=[
                pl.BlockSpec((1, tokens, width), lambda i, own: (early(i), 0, 0)),
                whole(first),
                whole(vec),
                weight_spec(gathered, lambda i, own: (early(i), CO)),
                weight_spec(gathered_mlp, lambda i, own: late(i)),
                weight_spec(gathered_mlp, lambda i, own: (late(i)[0], blocks + late(i)[1])),
                pl.BlockSpec((1, 1, 1, width), lambda i, own: (*late(i), 0, 0)),
            ],
            out_specs=[whole(first), whole(first), unit_spec, unit_spec, whole(half), whole(half)],
            scratch_shapes=[pltpu.VMEM(first.shape, F32)],
        ),
        out_shape=[struct(first.shape, F32), struct(first.shape, BF), units, units, half, half],
        compiler_params=compiler_params(1),
        cost_estimate=cost(tokens * D * columns * width * (2 + 4 * blocks), first, units, units, gathered_mlp),
        name="mlp_forward",
    )(own, mixed, first, vec, gathered, gathered_mlp, gathered_mlp, bias)


def mlp_back_kernel(
    grad_ref, second_ref, vec_ref, wd_ref, wu_ref, wo_ref, slope_ref,
    before_ref, unit_sum_ref, grad_second_ref, low_ref, sums_ref, mixed_ref, total_ref,
):
    step, columns = pl.program_id(0), mixed_ref.shape[1] * 0 + vec_ref.shape[1] // mixed_ref.shape[2]
    last = pl.num_programs(0) - columns

    @pl.when(step == 0)
    def _():
        total_ref[...] = jnp.zeros_like(total_ref)

    @pl.when(step < last)
    def _():
        grad_act = nn(grad_ref[...], weight(wd_ref))
        before = (grad_act * slope_ref[0, 0].astype(F32)).astype(BF)
        before_ref[0, 0] = before
        unit_sum_ref[0, 0] = jnp.sum(before.astype(F32), axis=0, keepdims=True)
        total_ref[...] += nt(before, weight(wu_ref))

    @pl.when(step == last - 1)
    def _():
        def finish(rows, back):
            incoming = grad_ref[rows, :].astype(F32)
            value = incoming + back
            grad_second_ref[rows, :] = value
            low_ref[rows, :] = value.astype(BF)
            return value.astype(BF)

        write_norm_back(total_ref, second_ref, vec_ref[2:3, :], sums_ref, finish)
        sums_ref[3:4, :] = jnp.sum(grad_ref[...].astype(F32), axis=0, keepdims=True)

    @pl.when(step >= last)
    def _():
        mixed_ref[0] = nn(low_ref[...], weight(wo_ref)).astype(BF)


def mlp_backward(grad, second, vec, gathered, gathered_mlp, slope):
    columns, blocks, tokens, width = slope.shape

    def early(i):
        rest = jnp.minimum(i, columns * blocks - 1)
        return rest // blocks, rest % blocks

    def late(i):
        return jnp.maximum(i - columns * blocks, 0)

    unit_spec = pl.BlockSpec((1, 1, tokens, width), lambda i: (*early(i), 0, 0))
    sums = struct((8, D), F32)
    return pl.pallas_call(
        mlp_back_kernel,
        grid=(columns * blocks + columns,),
        in_specs=[
            whole(grad),
            whole(second),
            whole(vec),
            weight_spec(gathered_mlp, lambda i: (early(i)[0], blocks + early(i)[1])),
            weight_spec(gathered_mlp, lambda i: early(i)),
            weight_spec(gathered, lambda i: (late(i), CO)),
            unit_spec,
        ],
        out_specs=[
            unit_spec,
            pl.BlockSpec((1, 1, 1, width), lambda i: (*early(i), 0, 0)),
            whole(second),
            whole(grad),
            whole(sums),
            pl.BlockSpec((1, tokens, width), lambda i: (late(i), 0, 0)),
        ],
        out_shape=[
            struct(slope.shape, BF),
            struct((columns, blocks, 1, width), F32),
            struct(second.shape, F32),
            struct(grad.shape, BF),
            sums,
            struct((columns, tokens, width), BF),
        ],
        scratch_shapes=[pltpu.VMEM(second.shape, F32)],
        compiler_params=compiler_params(1),
        cost_estimate=cost(tokens * D * columns * width * (2 + 4 * blocks), second, slope, slope, gathered_mlp),
        name="mlp_backward",
    )(grad, second, vec, gathered_mlp, gathered_mlp, gathered, slope)


def cross_back_kernel(q_ref, kv_ref, mixed_ref, grad_ref, probs_ref, query_ref, pair_ref, sums_ref):
    grad_query, grad_key, grad_value = attend_back(
        q_ref[0], kv_ref[0, 0, 0], kv_ref[0, 1, 0], mixed_ref[0], grad_ref[0], probs_ref
    )
    query_ref[0] = grad_query
    pair_ref[0, 0, 0] = grad_key
    pair_ref[0, 1, 0] = grad_value

    @pl.when(pl.program_id(2) == 0)
    def _():
        sums_ref[...] = jnp.zeros_like(sums_ref)

    sums_ref[0, 0:1, :] += jnp.sum(grad_query.astype(F32), axis=0, keepdims=True)
    sums_ref[0, 1:2, :] += jnp.sum(grad_value.astype(F32), axis=0, keepdims=True)


def attend_cross_back(query, pair, mixed, grad, probs):
    columns, tokens, width = query.shape
    seqs, length, pairs = pair.shape[2], pair.shape[3], width // LANES
    row_spec = pl.BlockSpec((1, LEN, LANES), lambda y, p, s: (y, s, p))
    pair_spec = pl.BlockSpec((1, 2, 1, length, LANES), lambda y, p, s: (y, 0, s, 0, p))
    return pl.pallas_call(
        cross_back_kernel,
        grid=(columns, pairs, seqs),
        in_specs=[
            row_spec,
            pair_spec,
            row_spec,
            row_spec,
            pl.BlockSpec((1, 1, 1, 2, length, LEN), lambda y, p, s: (y, p, s, 0, 0, 0)),
        ],
        out_specs=[row_spec, pair_spec, pl.BlockSpec((1, 8, LANES), lambda y, p, s: (y, 0, p))],
        out_shape=[
            struct(query.shape, BF),
            struct(pair.shape, BF),
            struct((columns, 8, width), F32),
        ],
        compiler_params=compiler_params(3),
        cost_estimate=cost(32 * columns * pairs * seqs * LEN * length * LANES, pair, pair, probs),
        name="attend_cross_back",
    )(query, pair, mixed, grad, probs)


def self_back_kernel(
    q_ref, k_ref, v_ref, mixed_ref, grad_ref, probs_ref, out_ref, sums_ref
):
    grad_query, grad_key, grad_value = attend_back(
        q_ref[0, 0], k_ref[0, 0], v_ref[0, 0], mixed_ref[0], grad_ref[0], probs_ref
    )
    out_ref[0, 0] = grad_query
    out_ref[0, 1] = grad_key
    out_ref[0, 2] = grad_value

    @pl.when(pl.program_id(2) == 0)
    def _():
        sums_ref[...] = jnp.zeros_like(sums_ref)

    sums_ref[0, 0:1, :] += jnp.sum(grad_query.astype(F32), axis=0, keepdims=True)
    sums_ref[0, 1:2, :] += jnp.sum(grad_value.astype(F32), axis=0, keepdims=True)


def attend_self_back(qkv, mixed, grad, probs):
    columns, _, tokens, width = qkv.shape
    seqs, pairs = probs.shape[2], width // LANES
    row_spec = pl.BlockSpec((1, LEN, LANES), lambda y, p, s: (y, s, p))

    def part(c):
        return pl.BlockSpec((1, 1, LEN, LANES), lambda y, p, s: (y, c, s, p))

    return pl.pallas_call(
        self_back_kernel,
        grid=(columns, pairs, seqs),
        in_specs=[
            part(0),
            part(1),
            part(2),
            row_spec,
            row_spec,
            pl.BlockSpec((1, 1, 1, 2, LEN, LEN), lambda y, p, s: (y, p, s, 0, 0, 0)),
        ],
        out_specs=[
            pl.BlockSpec((1, 3, LEN, LANES), lambda y, p, s: (y, 0, s, p)),
            pl.BlockSpec((1, 8, LANES), lambda y, p, s: (y, 0, p)),
        ],
        out_shape=[struct(qkv.shape, BF), struct((columns, 8, width), F32)],
        compiler_params=compiler_params(3),
        cost_estimate=cost(32 * columns * pairs * seqs * LEN * LEN * LANES, qkv, qkv, probs),
        name="attend_self_back",
    )(qkv, qkv, qkv, mixed, grad, probs)


def query_back_kernel(
    grad_ref, first_ref, second_ref, vec_ref, wq_ref, wo_ref,
    grad_first_ref, low_ref, sums_ref, mixed_ref, total_ref,
):
    step, columns = pl.program_id(0), pl.num_programs(0) // 2

    @pl.when(step == 0)
    def _():
        total_ref[...] = jnp.zeros_like(total_ref)

    @pl.when(step < columns)
    def _():
        total_ref[...] += nt(grad_ref[0], weight(wq_ref))

    @pl.when(step == columns - 1)
    def _():
        def finish(rows, back):
            value = second_ref[rows, :] + back
            grad_first_ref[rows, :] = value
            low_ref[rows, :] = value.astype(BF)
            return value.astype(BF)

        write_norm_back(total_ref, first_ref, vec_ref[1:2, :], sums_ref, finish)

    @pl.when(step >= columns)
    def _():
        mixed_ref[0] = nn(low_ref[...], weight(wo_ref)).astype(BF)


def query_backward(grad, first, grad_second, vec, gathered):
    columns, tokens, width = grad.shape

    def early(i):
        return jnp.minimum(i, columns - 1)

    def late(i):
        return jnp.maximum(i - columns, 0)

    sums = struct((8, D), F32)
    return pl.pallas_call(
        query_back_kernel,
        grid=(2 * columns,),
        in_specs=[
            pl.BlockSpec((1, tokens, width), lambda i: (early(i), 0, 0)),
            whole(first),
            whole(first),
            whole(vec),
            weight_spec(gathered, lambda i: (early(i), CQ)),
            weight_spec(gathered, lambda i: (late(i), OUT)),
        ],
        out_specs=[
            whole(first),
            whole(first),
            whole(sums),
            pl.BlockSpec((1, tokens, width), lambda i: (late(i), 0, 0)),
        ],
        out_shape=[struct(first.shape, F32), struct(first.shape, BF), sums, struct(grad.shape, BF)],
        scratch_shapes=[pltpu.VMEM(first.shape, F32)],
        compiler_params=compiler_params(1),
        cost_estimate=cost(4 * tokens * D * columns * width, first, first, first, grad),
        name="query_backward",
    )(grad, first, grad_second, vec, gathered, gathered)


def hidden_back_kernel(
    own_ref, grad_ref, hidden_ref, first_ref, vec_ref, w_ref, send_ref, keep_ref, sums_ref, total_ref
):
    step = pl.program_id(0)

    @pl.when(step == 0)
    def _():
        total_ref[...] = jnp.zeros_like(total_ref)

    total_ref[...] += nt(grad_ref[0, 0], weight(w_ref))

    @pl.when(step == pl.num_programs(0) - 1)
    def _():
        def finish(rows, back):
            value = first_ref[rows, :] + back
            send, keep = halves_of(value, own_ref[0])
            send_ref[rows, :] = send.astype(BF)
            keep_ref[rows, :] = keep
            return value

        write_norm_back(total_ref, hidden_ref, vec_ref[0:1, :], sums_ref, finish)


def hidden_backward(own, grad, hidden, grad_first, vec, gathered):
    columns, _, tokens, width = grad.shape
    sums, half = struct((8, D), F32), struct((tokens, width), F32)
    return pl.pallas_call(
        hidden_back_kernel,
        grid_spec=pltpu.PrefetchScalarGridSpec(
            num_scalar_prefetch=1,
            grid=(3 * columns,),
            in_specs=[
                pl.BlockSpec((1, 1, tokens, width), lambda i, own: (i // 3, i % 3, 0, 0)),
                whole(hidden),
                whole(grad_first),
                whole(vec),
                weight_spec(gathered, lambda i, own: (i // 3, QKV + i % 3)),
            ],
            out_specs=[whole(half), whole(half), whole(sums)],
            scratch_shapes=[pltpu.VMEM(hidden.shape, F32)],
        ),
        out_shape=[struct((tokens, width), BF), half, sums],
        compiler_params=compiler_params(1),
        cost_estimate=cost(6 * tokens * D * columns * width, grad, grad_first, hidden, grad_first),
        name="hidden_backward",
    )(own, grad, hidden, grad_first, vec, gathered)


def frames_back_kernel(own_ref, grad_ref, w_ref, send_ref, keep_ref, total_ref):
    step = pl.program_id(1)
    part = nt(grad_ref[0, 0, 0], weight(w_ref))

    @pl.when(step == 0)
    def _():
        total_ref[...] = part

    @pl.when(step > 0)
    def _():
        total_ref[...] += part

    @pl.when(step == pl.num_programs(1) - 1)
    def _():
        send, keep = halves_of(total_ref[...], own_ref[0])
        length, width = keep.shape
        for ref, value in ((send_ref, send), (keep_ref, keep)):
            ref[0, :length] = value.astype(BF)
            ref[0, length:] = jnp.zeros((ref.shape[1] - length, width), BF)


def frames_backward(own, grad, gathered):
    columns, _, seqs, length, width = grad.shape
    padded = -(-length // 16) * 16
    half = struct((seqs, padded, width), BF)
    half_spec = pl.BlockSpec((1, padded, width), lambda s, i, own: (s, 0, 0))
    return pl.pallas_call(
        frames_back_kernel,
        grid_spec=pltpu.PrefetchScalarGridSpec(
            num_scalar_prefetch=1,
            grid=(seqs, 2 * columns),
            in_specs=[
                pl.BlockSpec((1, 1, 1, length, width), lambda s, i, own: (i // 2, i % 2, s, 0, 0)),
                weight_spec(gathered, lambda s, i, own: (i // 2, CKV + i % 2)),
            ],
            out_specs=[half_spec, half_spec],
            scratch_shapes=[pltpu.VMEM((length, columns * width), F32)],
        ),
        out_shape=[half, half],
        compiler_params=compiler_params(2),
        cost_estimate=cost(4 * seqs * length * D * columns * width, grad, grad),
        name="frames_backward",
    )(own, grad, gathered)


class Plan:
    def __init__(self, order, bits):
        self.order, self.rest, self.bits = order, 1 << (bits - 2), bits
        self.sizes = {"x": 2, "y": 2, "z": self.rest}
        self.cuts = tuple(self.sizes[c] for c in order)

    def block(self, step_index):
        return tuple(1 if c == "y" else self.sizes[c] for c in self.order)

    def place(self, column):
        return tuple(column if c == "y" else 0 for c in self.order)

    def store(self, ref, value):
        rows = value.shape[0] // (2 * self.rest)
        value = value.reshape(2, self.rest, rows, value.shape[1])
        if self.order.index("x") > self.order.index("z"):
            value = value.swapaxes(0, 1)
        at = tuple(0 if c == "y" else slice(None) for c in self.order)
        ref[at + (0,)] = value


def cut_rows(place_ref, source, turned_ref, shards):
    rows = source.shape[0] // shards
    for shard in range(shards):
        at = pl.multiple_of(place_ref[1 + shard] * rows, rows)
        turned_ref[pl.ds(at, rows), :] = source[shard * rows : (shard + 1) * rows]


def weight_kernel(plan, frames, place_ref, left_ref, right_ref, send_ref, keep_ref, turned_ref):
    shards = 1 << plan.bits

    @pl.when((pl.program_id(0) == 0) & (pl.program_id(1) == 0))
    def _():
        if frames:
            for s in range(left_ref.shape[0]):
                cut_rows(place_ref, left_ref[s].T, turned_ref.at[s], shards)
        else:
            cut_rows(place_ref, left_ref[...].T, turned_ref, shards)

    if frames:
        total = 0.0
        for s in range(left_ref.shape[0]):
            total = total + nn(turned_ref[s], right_ref[0, 0, s])
    else:
        total = nn(turned_ref[...], right_ref[0, 0])
    half = total.shape[0] // 2
    plan.store(send_ref, total[:half].astype(BF))
    plan.store(keep_ref, total[half:].astype(BF))


def weight_grad(plan, place, left, right, frames=False, first=0, count=None):
    columns, blocks = right.shape[:2]
    blocks = count or blocks
    width = right.shape[-1]
    tokens = right.shape[-2]
    seqs = right.shape[2] if frames else 1
    rows = D >> plan.bits
    part = struct(plan.cuts + (blocks, rows, width), BF)
    out_spec = pl.BlockSpec(
        plan.block(0) + (1, rows, width),
        lambda y, i, place: plan.place(y) + (i, 0, 0),
    )

    def column(y, place):
        return jnp.where(y == 1, place[0], 1 - place[0])

    if frames:
        left_spec = whole(left)
        right_spec = pl.BlockSpec(
            (1, 1, seqs, tokens, width), lambda y, i, place: (column(y, place), first + i, 0, 0, 0)
        )
        turned = pltpu.VMEM((seqs, D, tokens), BF)
    else:
        left_spec = whole(left)
        right_spec = pl.BlockSpec((1, 1, tokens, width), lambda y, i, place: (column(y, place), first + i, 0, 0))
        turned = pltpu.VMEM((D, tokens), BF)
    return pl.pallas_call(
        functools.partial(weight_kernel, plan, frames),
        grid_spec=pltpu.PrefetchScalarGridSpec(
            num_scalar_prefetch=1,
            grid=(columns, blocks),
            in_specs=[left_spec, right_spec],
            out_specs=[out_spec, out_spec],
            scratch_shapes=[turned],
        ),
        out_shape=[part, part],
        compiler_params=compiler_params(2),
        cost_estimate=cost(2 * columns * blocks * seqs * tokens * width * D, right, part, part),
        name="weight_grad",
    )(place, left, right)


def cut_kernel(keep_ref, got_ref, send_ref, out_ref):
    for part, ref in ((0, send_ref), (1, out_ref)):
        ref[...] = (keep_ref[part].astype(F32) + got_ref[part].astype(F32)).astype(BF)


def add_and_cut(keep, got):
    shape = keep.shape[1:]
    width = shape[-1]
    rows = math.prod(shape[:-1])
    step = math.gcd(rows, 1024)
    flat = (2, rows, width)
    out = struct((rows, width), BF)
    in_spec = pl.BlockSpec((2, step, width), lambda i: (0, i, 0))
    out_spec = pl.BlockSpec((step, width), lambda i: (i, 0))
    send, own = pl.pallas_call(
        cut_kernel,
        grid=(rows // step,),
        in_specs=[in_spec, in_spec],
        out_specs=[out_spec, out_spec],
        out_shape=[out, out],
        compiler_params=compiler_params(1),
        cost_estimate=cost(0, keep, got, out, out),
        name="add_and_cut",
    )(keep.reshape(flat), got.reshape(flat))
    return send.reshape(shape), own.reshape(shape)


def frames_join_kernel(own_ref, keep_ref, *refs):
    *got_refs, out_ref = refs
    length, seqs = out_ref.shape[0], len(got_refs)
    for s in range(seqs):
        keep = keep_ref[s, :length].astype(F32)
        got = got_refs[s][0, :length].astype(F32)
        out_ref[:, s, :] = jnp.where(own_ref[0] == 0, keep, got)
        out_ref[:, seqs + s, :] = jnp.where(own_ref[0] == 0, got, keep)


def join_frames(own, keep, *arguments):
    *got, length = arguments
    seqs, padded, width = keep.shape
    return pl.pallas_call(
        frames_join_kernel,
        grid_spec=pltpu.PrefetchScalarGridSpec(
            num_scalar_prefetch=1,
            grid=(width // LANES,),
            in_specs=[pl.BlockSpec((seqs, padded, LANES), lambda i, own: (0, 0, i))]
            + [pl.BlockSpec((1, padded, LANES), lambda i, own: (0, 0, i))] * seqs,
            out_specs=pl.BlockSpec((length, 2 * seqs, LANES), lambda i, own: (0, 0, i)),
        ),
        out_shape=struct((length, 2 * seqs, width), F32),
        compiler_params=compiler_params(1),
        cost_estimate=cost(0, keep),
        name="join_frames",
    )(own, keep, *got)


def swap(axis, bit, value):
    size = lax.axis_size(axis)
    return lax.ppermute(value, axis, [(d, d ^ (1 << bit)) for d in range(size)])


def pick(array, index, axis):
    return lax.dynamic_index_in_dim(array, index, axis, keepdims=False)


def exchange(keep, send):
    if lax.axis_size("tp") != 2:
        got = lax.all_to_all(send, "tp", split_axis=0, concat_axis=0, tiled=True)
        return got.astype(keep.dtype)
    own = lax.axis_index("tp")
    got = swap("tp", 0, pick(send, 1 - own, 0)).astype(keep.dtype)
    mine = pick(keep, own, 0)
    return jnp.where(own == 0, jnp.stack([mine, got]), jnp.stack([got, mine]))


def bits_of(axis):
    return lax.axis_size(axis).bit_length() - 1


class Chain:
    def __init__(self):
        self.token = None

    def tie(self, *values):
        if self.token is None:
            return values
        return lax.optimization_barrier((*values, self.token))[:-1]

    def hold(self, value):
        (self.token,) = self.tie(value)
        return self.token


class Reduction:
    def __init__(self, chain, plan, place, left, right, **options):
        self.chain, self.result = chain, None
        stages = {"x": [("dp", 1)], "y": [("tp", 0)], "z": [("dp", b) for b in range(2, plan.bits)]}
        self.order = [stage for c in plan.order for stage in stages[c]]
        (right,) = chain.tie(right)
        send, keep = weight_grad(plan, place, left, right, **options)
        chain.token = send
        self.cuts = []
        for c in plan.order:
            self.cuts += [2] * len(stages[c])
        shape = tuple(self.cuts) + send.shape[len(plan.cuts) :]
        self.keep, self.first, self.got = keep.reshape(shape), send.reshape(shape), None

    def step(self):
        if self.got is None:
            self.got = swap("dp", 0, self.chain.tie(self.first)[0])
        elif self.order:
            keep, got = self.chain.tie(self.keep, self.got)
            send, self.keep = add_and_cut(keep, got)
            self.chain.token = send
            self.got = swap(*self.order.pop(0), send)
        elif self.result is None:
            keep, got = self.chain.tie(self.keep, self.got)
            self.result = keep.astype(F32) + got.astype(F32)

    def finish(self):
        while self.result is None:
            self.step()
        return self.result


def per_device_whole_sequences(
    hidden_in, encoder_states, positions, self_qkv, self_out, cross_query, cross_kv, cross_out,
    up_weight, down_weight, norm_gains, bias_rows, up_bias, out_grad,
):
    columns, shards = lax.axis_size("tp"), lax.axis_size("dp")
    own = lax.axis_index("tp")
    width = hidden_in.shape[1]
    tokens = hidden_in.shape[0] // columns
    seqs = positions.shape[0] // columns
    own_index = own.astype(jnp.int32).reshape(1)

    attention_part = jnp.concatenate(
        [
            self_qkv.transpose(1, 0, 2),
            cross_kv.transpose(1, 0, 2),
            self_out.T[None],
            cross_query[None],
            cross_out.T[None],
        ]
    )
    rows = up_weight.shape[0]
    blocks = up_weight.shape[1] // width
    mlp_part = jnp.concatenate(
        [
            up_weight.reshape(rows, blocks, width).transpose(1, 0, 2),
            down_weight.reshape(blocks, width, rows).transpose(0, 2, 1),
        ]
    )

    def gather(part):
        full = lax.all_gather(part, ("tp", "dp"), axis=0)
        return full.reshape((columns, shards) + part.shape)

    weights, weights_mlp = gather(attention_part), gather(mlp_part)

    def to_tokens(array):
        mine = lax.dynamic_slice_in_dim(array, own * tokens, tokens, 0)
        got = swap("tp", 0, lax.dynamic_slice_in_dim(array, (1 - own) * tokens, tokens, 0))
        return jnp.where(
            own == 0, jnp.concatenate([mine, got], axis=1), jnp.concatenate([got, mine], axis=1)
        )

    hidden, grad_final = to_tokens(hidden_in), to_tokens(out_grad)
    small = jnp.concatenate([norm_gains, bias_rows, up_bias.reshape(blocks, width)])
    every = jnp.broadcast_to(small, (columns,) + small.shape)
    every = exchange(every, every)
    vec = every[:, :13].transpose(1, 0, 2).reshape(13, columns * width)
    vec = jnp.concatenate([vec, jnp.zeros((3, columns * width), F32)])
    none = jnp.zeros((columns, width), F32)
    bias = lambda row: every[:, 3 + row]
    qkv_bias = jnp.stack([bias(3), none, bias(4)], axis=1)[:, :, None]
    pair_bias = jnp.stack([none, bias(7)], axis=1)[:, :, None]
    up_rows = every[:, 13:][:, :, None]
    order = lax.dynamic_slice_in_dim(positions, own * seqs, seqs, 0)

    frames = lax.optimization_barrier(
        lax.dynamic_slice_in_dim(encoder_states, own * seqs, seqs, 0)
    )

    qkv, normed_a = project_qkv(hidden, vec, weights, qkv_bias)
    pair = project_pair(own_index, frames, weights, pair_bias, seqs)
    mixed_a, probs_a = attend_self(qkv, order[:, None, :], order[:, :, None])
    first, normed_c, query = project_out(mixed_a, hidden, vec, weights, bias(6)[:, None])
    mixed_c, probs_c = attend_cross(query, pair)
    second, normed_m, activated, slope, send_output, keep_output = mlp_forward(
        own_index, mixed_c, first, vec, weights, weights_mlp, up_rows
    )

    got_output = swap("tp", 0, send_output)

    def pair_up(keep, got):
        got = got.astype(keep.dtype)
        return jnp.where(own == 0, jnp.stack([keep, got]), jnp.stack([got, keep]))

    chain = Chain()
    chain.token = send_output
    bits = bits_of("dp")
    device = lax.axis_index("dp")
    shard = jnp.arange(shards)
    same = ~(shard ^ device)
    spot = sum(((same >> b) & 1) << (bits - 1 - b) for b in range(bits))
    place = jnp.concatenate([own_index, spot.astype(jnp.int32)])

    def reduction(left, right, order="xyz", **options):
        return Reduction(chain, Plan(order, bits), place, left, right, **options)

    def advance(*several):
        for one in several:
            one.step()

    def run(kernel, first_array, *arrays):
        (first_array,) = chain.tie(first_array)
        results = kernel(first_array, *arrays)
        chain.token = results[0]
        return results

    down = reduction(grad_final, activated)
    advance(down)
    grad_before, up_sums, grad_second, low_second, sums_m, grad_mixed_c = run(
        mlp_backward, grad_final, second, vec, weights, weights_mlp, slope
    )
    output = pair_up(keep_output, chain.hold(got_output)).reshape(columns * tokens, width)
    advance(down)
    up = reduction(normed_m, grad_before, "yxz")
    advance(up)
    co = reduction(low_second, mixed_c[:, None], "zyx")
    advance(up, co)
    (grad_mixed_c,) = chain.tie(grad_mixed_c)
    grad_query, grad_pair, sums_cross = run(attend_cross_back, query, pair, mixed_c, grad_mixed_c, probs_c)
    advance(down, up, co)
    send_frames, keep_frames = run(
        lambda grad: frames_backward(own_index, grad, weights), grad_pair
    )
    advance(down, up, co)
    got_frames = [swap("tp", 0, part) for part in jnp.split(chain.tie(send_frames)[0], seqs)]
    kv = reduction(frames, grad_pair, "xzy", frames=True)
    got_frames[0] = chain.hold(got_frames[0])
    grad_first, low_first, sums_c, grad_mixed_a = run(
        query_backward, grad_query, first, grad_second, vec, weights
    )
    advance(down, up, co, kv)
    (grad_mixed_a,) = chain.tie(grad_mixed_a)
    grad_triple, sums_self = run(attend_self_back, qkv, mixed_a, grad_mixed_a, probs_a)
    advance(co, kv)
    triple = reduction(normed_a, grad_triple, "xyz", first=0, count=2)
    values = reduction(normed_a, grad_triple, "yxz", first=2, count=1)
    got_frames[1:] = [chain.hold(part) for part in got_frames[1:]]
    advance(kv, triple, values)
    cq = reduction(normed_c, grad_query[:, None], "zxy")
    advance(triple, values, cq)
    out = reduction(low_first, mixed_a[:, None], "zyx")
    advance(kv, cq, out)
    send_hidden, keep_hidden, sums_a = run(
        lambda grad: hidden_backward(own_index, grad, hidden, grad_first, vec, weights), grad_triple
    )
    got_hidden = swap("tp", 0, chain.tie(send_hidden)[0])

    halves = lambda row: row.reshape(columns, width)
    gains = [halves(sums[0]) for sums in (sums_a, sums_c, sums_m)]
    shifts = [halves(sums[1]) for sums in (sums_a, sums_c, sums_m)]
    sums = jnp.stack(
        gains
        + shifts
        + [
            sums_self[:, 0],
            sums_self[:, 1],
            halves(sums_c[2]),
            sums_cross[:, 0],
            sums_cross[:, 1],
            halves(sums_m[2]),
            halves(sums_m[3]),
        ],
        axis=1,
    )
    totals = jnp.concatenate([sums, up_sums[:, :, 0]], axis=1)
    def spread(totals, bit):
        return totals + chain.hold(swap("dp", bit, totals))

    totals = spread(totals, 0)
    advance(triple, values)
    encoder_grad = join_frames(own_index, keep_frames, *got_frames, frames.shape[1])
    chain.token = encoder_grad
    advance(out, cq)
    hidden_grad = pair_up(keep_hidden, chain.hold(got_hidden)).reshape(columns * tokens, width)
    chain.hold(hidden_grad)
    for bit in range(1, bits):
        totals = spread(totals, bit)
        advance(triple, values, out, cq)
    totals = pick(totals, own, 0) + swap("tp", 0, pick(totals, 1 - own, 0))
    encoder_grad = encoder_grad.transpose(1, 0, 2)
    own_qkv = jnp.concatenate([triple.finish(), values.finish()])
    own_ckv, own_cq, own_out = kv.finish(), cq.finish(), out.finish()
    own_down, own_up, own_co = down.finish(), up.finish(), co.finish()

    return (
        output,
        hidden_grad,
        encoder_grad,
        own_qkv.transpose(1, 0, 2),
        own_out[0].T,
        own_cq[0],
        own_ckv.transpose(1, 0, 2),
        own_co[0].T,
        own_up.transpose(1, 0, 2).reshape(rows, blocks * width),
        own_down.transpose(0, 2, 1).reshape(blocks * width, rows),
        totals[:3],
        totals[3:13],
        totals[13:].reshape(blocks * width),
    )


def to_heads(matrix, groups):
    return matrix.reshape(groups, -1, matrix.shape[-1] // HEAD_DIM, HEAD_DIM)


def norm_forward(values, gain, shift):
    row_sum, square_sum = lax.psum(
        (jnp.sum(values, axis=1), jnp.sum(values * values, axis=1)), "tp"
    )
    width = values.shape[1] * lax.axis_size("tp")
    row_mean = row_sum / width
    inverse = lax.rsqrt(square_sum / width - row_mean * row_mean + EPSILON)
    unit = (values - row_mean[:, None]) * inverse[:, None]
    normed = (unit * gain + shift).astype(jnp.bfloat16)
    return (lax.all_gather(normed, "tp", axis=1, tiled=True), unit, inverse)


def norm_backward(incoming, unit, inverse, gain):
    scaled = incoming * gain
    first_sum, second_sum = lax.psum(
        (jnp.sum(scaled, axis=1), jnp.sum(scaled * unit, axis=1)), "tp"
    )
    width = incoming.shape[1] * lax.axis_size("tp")
    outgoing = inverse[:, None] * (
        scaled - first_sum[:, None] / width - unit * (second_sum[:, None] / width)
    )
    return (outgoing, jnp.sum(incoming * unit, axis=0), jnp.sum(incoming, axis=0))


def branch_total(partial_value):
    return lax.psum_scatter(partial_value, "tp", scatter_dimension=1, tiled=True)


def spread_grad(incoming):
    return lax.all_gather(incoming.astype(jnp.bfloat16), "tp", axis=1, tiled=True)


def spread_heads(columns):
    return lax.all_gather(columns, "tp", axis=1, tiled=True)


def input_total(partial_value):
    return lax.psum_scatter(partial_value, "tp", scatter_dimension=1, tiled=True)


def scores_of(query, key_rows, visible):
    scores = jnp.einsum(
        "sqhe,skhe->shqk", query, key_rows, preferred_element_type=jnp.float32
    ) * HEAD_DIM ** (-0.5)
    if visible is None:
        return scores
    return jnp.where(visible[:, None], scores, NEGATIVE)


def attend_forward(query, key_rows, value_rows, visible):
    scores = scores_of(query, key_rows, visible)
    row_max = jnp.max(scores, axis=-1, keepdims=True)
    weights = jnp.exp(scores - row_max)
    row_total = jnp.sum(weights, axis=-1, keepdims=True)
    probs = (weights / row_total).astype(jnp.bfloat16)
    mixed = jnp.einsum("shqk,skhe->sqhe", probs, value_rows, preferred_element_type=jnp.float32)
    return (mixed.astype(jnp.bfloat16), row_max + jnp.log(row_total))


def attend_backward(query, key_rows, value_rows, visible, log_total, grad_mixed):
    weights = jnp.exp(scores_of(query, key_rows, visible) - log_total)
    grad_weights = jnp.einsum(
        "sqhe,skhe->shqk", grad_mixed, value_rows, preferred_element_type=jnp.float32
    )
    inner = jnp.sum(weights * grad_weights, axis=-1, keepdims=True)
    grad_scores = (weights * (grad_weights - inner)).astype(jnp.bfloat16)
    factor = HEAD_DIM ** (-0.5)
    grad_query = (
        jnp.einsum("shqk,skhe->sqhe", grad_scores, key_rows, preferred_element_type=jnp.float32)
        * factor
    )
    grad_key = (
        jnp.einsum("shqk,sqhe->skhe", grad_scores, query, preferred_element_type=jnp.float32)
        * factor
    )
    grad_value = jnp.einsum(
        "shqk,sqhe->skhe",
        weights.astype(jnp.bfloat16),
        grad_mixed,
        preferred_element_type=jnp.float32,
    )
    return (
        grad_query.astype(jnp.bfloat16),
        grad_key.astype(jnp.bfloat16),
        grad_value.astype(jnp.bfloat16),
    )


def column_sum(matrix):
    return jnp.sum(matrix, axis=0, dtype=jnp.float32)


def per_device(
    hidden_in,
    encoder_states,
    positions,
    self_qkv,
    self_out,
    cross_query,
    cross_kv,
    cross_out,
    up_weight,
    down_weight,
    norm_gains,
    bias_rows,
    up_bias,
    out_grad,
):
    local_width = hidden_in.shape[1]
    local_units = up_weight.shape[1]
    group_rows = SEQ_MB * LEN
    zeros_f = jnp.float32
    grad_qkv = jnp.zeros((D, 3, local_width), zeros_f)
    grad_out = jnp.zeros((local_width, D), zeros_f)
    grad_cq = jnp.zeros((D, local_width), zeros_f)
    grad_ckv = jnp.zeros((D, 2, local_width), zeros_f)
    grad_co = jnp.zeros((local_width, D), zeros_f)
    grad_up = jnp.zeros((D, local_units), zeros_f)
    grad_down = jnp.zeros((local_units, D), zeros_f)
    gain_terms = jnp.zeros((3, local_width), zeros_f)
    bias_terms = jnp.zeros((10, local_width), zeros_f)
    upbias_terms = jnp.zeros((local_units,), zeros_f)
    outputs = []
    hidden_grads = []
    encoder_grads = []
    for batch_index in range(MICRO):
        weights_now = (
            lax.all_gather(self_qkv, "dp", axis=0, tiled=True),
            lax.all_gather(self_out, "dp", axis=1, tiled=True),
            lax.all_gather(cross_query, "dp", axis=0, tiled=True),
            lax.all_gather(cross_kv, "dp", axis=0, tiled=True),
            lax.all_gather(cross_out, "dp", axis=1, tiled=True),
            lax.all_gather(up_weight, "dp", axis=0, tiled=True),
            lax.all_gather(down_weight, "dp", axis=1, tiled=True),
        )
        qkv_full, out_full, cq_full, ckv_full, co_full, up_full, down_full = weights_now
        self_columns, cross_columns, query_transposed = (
            lax.all_to_all(out_full, "tp", split_axis=1, concat_axis=0, tiled=True),
            lax.all_to_all(co_full, "tp", split_axis=1, concat_axis=0, tiled=True),
            lax.all_to_all(cq_full.T, "tp", split_axis=1, concat_axis=0, tiled=True),
        )
        lower = batch_index * group_rows
        first_seq = batch_index * SEQ_MB
        resid = hidden_in[lower : lower + group_rows].astype(jnp.float32)
        frames = encoder_states[first_seq : first_seq + SEQ_MB]
        order = positions[first_seq : first_seq + SEQ_MB]
        visible = order[:, None, :] <= order[:, :, None]
        normed_a, unit_a, inverse_a = norm_forward(resid, norm_gains[0], bias_rows[0])
        triple = jnp.einsum("td,dcf->tcf", normed_a, qkv_full, preferred_element_type=jnp.float32)
        query = to_heads((triple[:, 0] + bias_rows[3]).astype(jnp.bfloat16), SEQ_MB)
        keys = to_heads(triple[:, 1].astype(jnp.bfloat16), SEQ_MB)
        values = to_heads((triple[:, 2] + bias_rows[4]).astype(jnp.bfloat16), SEQ_MB)
        mixed, log_self = attend_forward(query, keys, values, visible)
        mixed_rows = mixed.reshape(group_rows, local_width)
        self_share = jnp.dot(
            spread_heads(mixed_rows), self_columns, preferred_element_type=jnp.float32
        )
        first = resid + self_share + bias_rows[5]
        normed_c, unit_c, inverse_c = norm_forward(first, norm_gains[1], bias_rows[1])
        cross_q = to_heads(
            (jnp.dot(normed_c, cq_full, preferred_element_type=jnp.float32) + bias_rows[6]).astype(
                jnp.bfloat16
            ),
            SEQ_MB,
        )
        paired = jnp.einsum("sfd,dcg->sfcg", frames, ckv_full, preferred_element_type=jnp.float32)
        cross_k = to_heads(paired[:, :, 0].astype(jnp.bfloat16), SEQ_MB)
        cross_v = to_heads((paired[:, :, 1] + bias_rows[7]).astype(jnp.bfloat16), SEQ_MB)
        cross_mixed, log_cross = attend_forward(cross_q, cross_k, cross_v, None)
        cross_rows = cross_mixed.reshape(group_rows, local_width)
        cross_share = jnp.dot(
            spread_heads(cross_rows), cross_columns, preferred_element_type=jnp.float32
        )
        second = first + cross_share + bias_rows[8]
        normed_m, unit_m, inverse_m = norm_forward(second, norm_gains[2], bias_rows[2])
        before = jnp.dot(normed_m, up_full, preferred_element_type=jnp.float32) + up_bias
        activated = jax.nn.gelu(before, approximate=False).astype(jnp.bfloat16)
        final = (
            second
            + branch_total(jnp.dot(activated, down_full, preferred_element_type=jnp.float32))
            + bias_rows[9]
        )
        outputs.append(final.astype(jnp.bfloat16))
        weights_back = (
            lax.all_gather(self_qkv, "dp", axis=0, tiled=True),
            lax.all_gather(self_out, "dp", axis=1, tiled=True),
            lax.all_gather(cross_query, "dp", axis=0, tiled=True),
            lax.all_gather(cross_kv, "dp", axis=0, tiled=True),
            lax.all_gather(cross_out, "dp", axis=1, tiled=True),
            lax.all_gather(up_weight, "dp", axis=0, tiled=True),
            lax.all_gather(down_weight, "dp", axis=1, tiled=True),
        )
        qkv_back, out_back, cq_back, ckv_back, co_back, up_back, down_back = weights_back
        grad_final = out_grad[lower : lower + group_rows]
        grad_final_full = spread_grad(grad_final)
        grad_down = grad_down + jnp.einsum(
            "tf,td->fd", activated, grad_final_full, preferred_element_type=jnp.float32
        )
        grad_act = jnp.einsum(
            "td,fd->tf", grad_final_full, down_back, preferred_element_type=jnp.float32
        )
        normal_cdf = 0.5 * (1.0 + lax.erf(before / math.sqrt(2.0)))
        density = jnp.exp(-0.5 * before * before) / math.sqrt(2.0 * math.pi)
        grad_before = (grad_act * (normal_cdf + before * density)).astype(jnp.bfloat16)
        grad_up = grad_up + jnp.einsum(
            "td,tf->df", normed_m, grad_before, preferred_element_type=jnp.float32
        )
        grad_norm_m = input_total(
            jnp.einsum("tf,df->td", grad_before, up_back, preferred_element_type=jnp.float32)
        )
        back_m, gain_m, shift_m = norm_backward(grad_norm_m, unit_m, inverse_m, norm_gains[2])
        grad_second = grad_final.astype(jnp.float32) + back_m
        grad_cross_full = spread_grad(grad_second)
        grad_co = grad_co + jnp.einsum(
            "tg,td->gd", cross_rows, grad_cross_full, preferred_element_type=jnp.float32
        )
        grad_cross_mixed = to_heads(
            jnp.einsum(
                "td,gd->tg", grad_cross_full, co_back, preferred_element_type=jnp.float32
            ).astype(jnp.bfloat16),
            SEQ_MB,
        )
        grad_cq_heads, grad_ck_heads, grad_cv_heads = attend_backward(
            cross_q, cross_k, cross_v, None, log_cross, grad_cross_mixed
        )
        grad_cq_rows = grad_cq_heads.reshape(group_rows, local_width)
        grad_kv = jnp.stack(
            [
                grad_ck_heads.reshape(SEQ_MB, -1, local_width),
                grad_cv_heads.reshape(SEQ_MB, -1, local_width),
            ],
            axis=2,
        )
        grad_cq = grad_cq + jnp.einsum(
            "td,tg->dg", normed_c, grad_cq_rows, preferred_element_type=jnp.float32
        )
        grad_ckv = grad_ckv + jnp.einsum(
            "sfd,sfcg->dcg", frames, grad_kv, preferred_element_type=jnp.float32
        )
        frame_partial = jnp.einsum(
            "sfcg,dcg->sfd", grad_kv, ckv_back, preferred_element_type=jnp.float32
        )
        encoder_grads.append(
            lax.psum_scatter(
                frame_partial.astype(jnp.bfloat16), "tp", scatter_dimension=2, tiled=True
            ).astype(jnp.float32)
        )
        grad_norm_c = jnp.dot(
            spread_heads(grad_cq_rows), query_transposed, preferred_element_type=jnp.float32
        )
        back_c, gain_c, shift_c = norm_backward(grad_norm_c, unit_c, inverse_c, norm_gains[1])
        grad_first = grad_second + back_c
        grad_self_full = spread_grad(grad_first)
        grad_out = grad_out + jnp.einsum(
            "tg,td->gd", mixed_rows, grad_self_full, preferred_element_type=jnp.float32
        )
        grad_mixed = to_heads(
            jnp.einsum(
                "td,gd->tg", grad_self_full, out_back, preferred_element_type=jnp.float32
            ).astype(jnp.bfloat16),
            SEQ_MB,
        )
        grad_q_heads, grad_k_heads, grad_v_heads = attend_backward(
            query, keys, values, visible, log_self, grad_mixed
        )
        grad_triple = jnp.stack(
            [
                grad_q_heads.reshape(group_rows, local_width),
                grad_k_heads.reshape(group_rows, local_width),
                grad_v_heads.reshape(group_rows, local_width),
            ],
            axis=1,
        )
        grad_qkv = grad_qkv + jnp.einsum(
            "td,tcg->dcg", normed_a, grad_triple, preferred_element_type=jnp.float32
        )
        grad_norm_a = input_total(
            jnp.einsum("tcg,dcg->td", grad_triple, qkv_back, preferred_element_type=jnp.float32)
        )
        back_a, gain_a, shift_a = norm_backward(grad_norm_a, unit_a, inverse_a, norm_gains[0])
        hidden_grads.append(grad_first + back_a)
        gain_terms = gain_terms + jnp.stack([gain_a, gain_c, gain_m])
        bias_terms = bias_terms + jnp.stack(
            [
                shift_a,
                shift_c,
                shift_m,
                column_sum(grad_triple[:, 0]),
                column_sum(grad_triple[:, 2]),
                column_sum(grad_first.astype(jnp.bfloat16)),
                column_sum(grad_cq_rows),
                column_sum(grad_kv[:, :, 1].reshape(-1, local_width)),
                column_sum(grad_second.astype(jnp.bfloat16)),
                column_sum(grad_final),
            ]
        )
        upbias_terms = upbias_terms + column_sum(grad_before)
    weight_totals = (
        lax.psum_scatter(
            grad_qkv.astype(jnp.bfloat16), "dp", scatter_dimension=0, tiled=True
        ).astype(jnp.float32),
        lax.psum_scatter(
            grad_out.astype(jnp.bfloat16), "dp", scatter_dimension=1, tiled=True
        ).astype(jnp.float32),
        lax.psum_scatter(
            grad_cq.astype(jnp.bfloat16), "dp", scatter_dimension=0, tiled=True
        ).astype(jnp.float32),
        lax.psum_scatter(
            grad_ckv.astype(jnp.bfloat16), "dp", scatter_dimension=0, tiled=True
        ).astype(jnp.float32),
        lax.psum_scatter(
            grad_co.astype(jnp.bfloat16), "dp", scatter_dimension=1, tiled=True
        ).astype(jnp.float32),
        lax.psum_scatter(
            grad_up.astype(jnp.bfloat16), "dp", scatter_dimension=0, tiled=True
        ).astype(jnp.float32),
        lax.psum_scatter(
            grad_down.astype(jnp.bfloat16), "dp", scatter_dimension=1, tiled=True
        ).astype(jnp.float32),
    )
    vector_totals = lax.psum((gain_terms, bias_terms, upbias_terms), "dp")
    return (
        jnp.concatenate(outputs, axis=0),
        jnp.concatenate(hidden_grads, axis=0),
        jnp.concatenate(encoder_grads, axis=0),
        weight_totals[0],
        weight_totals[1],
        weight_totals[2],
        weight_totals[3],
        weight_totals[4],
        weight_totals[5],
        weight_totals[6],
        vector_totals[0],
        vector_totals[1],
        vector_totals[2],
    )


def solution(mesh):
    in_specs = (
        P("dp", "tp"),
        P("dp", None, None),
        P("dp", None),
        P("dp", None, "tp"),
        P("tp", "dp"),
        P("dp", "tp"),
        P("dp", None, "tp"),
        P("tp", "dp"),
        P("dp", "tp"),
        P("tp", "dp"),
        P(None, "tp"),
        P(None, "tp"),
        P("tp"),
        P("dp", "tp"),
    )
    out_specs = (
        P("dp", "tp"),
        P("dp", "tp"),
        P("dp", None, "tp"),
        P("dp", None, "tp"),
        P("tp", "dp"),
        P("dp", "tp"),
        P("dp", None, "tp"),
        P("tp", "dp"),
        P("dp", "tp"),
        P("tp", "dp"),
        P(None, "tp"),
        P(None, "tp"),
        P("tp"),
    )
    columns, shards = mesh.shape["tp"], mesh.shape["dp"]
    powers = columns & (columns - 1) == 0 and shards & (shards - 1) == 0

    def device_step(*arrays):
        seqs = arrays[2].shape[0]
        wide = arrays[0].shape[1] % LANES == 0
        if powers and wide and columns == 2 and seqs % columns == 0 and shards >= 8:
            return per_device_whole_sequences(*arrays)
        return per_device(*arrays)

    return jax.shard_map(
        device_step, mesh=mesh, in_specs=in_specs, out_specs=out_specs, check_vma=False
    )
```

```python
import functools
import math

import jax
import jax.numpy as jnp
from jax import lax
from jax.experimental import pallas as pl
from jax.experimental.pallas import tpu as pltpu
from jax.sharding import PartitionSpec as P

D = 1024
LEN = 448
SEQ_MB = 1
MICRO = 4
HEAD_DIM = 64
BF = jnp.bfloat16
F32 = jnp.float32
LANES = 128


EPSILON = 1e-05
NEGATIVE = -1e30

QKV, OUT, CKV, CQ, CO = 0, 3, 4, 6, 7
VMEM_BYTES = 58 << 20
SELF_LANES = 256


def nn(a, b):
    return jnp.dot(a, b, preferred_element_type=F32)


def nt(a, b):
    return lax.dot_general(a, b, (((1,), (1,)), ((), ())), preferred_element_type=F32)


def tn(a, b):
    return lax.dot_general(a, b, (((0,), (0,)), ((), ())), preferred_element_type=F32)


def compiler_params(axes):
    return pltpu.CompilerParams(
        dimension_semantics=("arbitrary",) * axes, vmem_limit_bytes=VMEM_BYTES
    )


def cost(flops, *arrays):
    time = (3e-6 + flops / 700e12) / 7
    return pl.CostEstimate(
        flops=int(time * 1153e12), bytes_accessed=int(time * 3690e9), transcendentals=0
    )


def struct(shape, dtype):
    return jax.ShapeDtypeStruct(shape, dtype)


def weight(ref):
    block = ref[0, :, 0]
    return block.reshape(block.shape[0] * block.shape[1], block.shape[2])


def weight_spec(gathered, index):
    _, shards, _, rows, width = gathered.shape

    def index_map(*grid):
        column, block = index(*grid)
        return (column, 0, block, 0, 0)

    return pl.BlockSpec((1, shards, 1, rows, width), index_map)


def whole(array):
    return pl.BlockSpec(array.shape, lambda *grid: (0,) * len(array.shape))


def row_loop(rows, body):
    step = 128 if rows % 128 == 0 else 64

    def run(at, carried):
        body(pl.ds(pl.multiple_of(at * step, step), step))
        return carried

    lax.fori_loop(0, rows // step, run, 0)


def norm_stats(values):
    row_mean = jnp.mean(values, axis=1, keepdims=True)
    square = jnp.mean(values * values, axis=1, keepdims=True)
    return row_mean, lax.rsqrt(square - row_mean * row_mean + EPSILON)


def write_norm(source_ref, normed_ref, gain, shift):
    def body(rows):
        values = source_ref[rows, :].astype(F32)
        row_mean, inverse = norm_stats(values)
        normed_ref[rows, :] = ((values - row_mean) * inverse * gain + shift).astype(BF)

    row_loop(source_ref.shape[0], body)


def write_norm_back(grad_ref, source_ref, gain, sums_ref, finish):
    sums_ref[...] = jnp.zeros_like(sums_ref)

    def body(rows):
        incoming = grad_ref[rows, :]
        values = source_ref[rows, :].astype(F32)
        row_mean, inverse = norm_stats(values)
        unit = (values - row_mean) * inverse
        scaled = incoming * gain
        back = inverse * (
            scaled
            - jnp.mean(scaled, axis=1, keepdims=True)
            - unit * jnp.mean(scaled * unit, axis=1, keepdims=True)
        )
        low = finish(rows, back)
        sums_ref[0:1, :] += jnp.sum(incoming * unit, axis=0, keepdims=True)
        sums_ref[1:2, :] += jnp.sum(incoming, axis=0, keepdims=True)
        sums_ref[2:3, :] += jnp.sum(low.astype(F32), axis=0, keepdims=True)

    row_loop(grad_ref.shape[0], body)


def first_norm_kernel(hidden_ref, vec_ref, normed_ref):
    write_norm(hidden_ref, normed_ref, vec_ref[0:1, :], vec_ref[3:4, :])


def first_norm(hidden, vec):
    return pl.pallas_call(
        first_norm_kernel,
        out_shape=struct(hidden.shape, BF),
        compiler_params=pltpu.CompilerParams(vmem_limit_bytes=VMEM_BYTES),
        cost_estimate=cost(0, hidden),
        name="first_norm",
    )(hidden, vec)


def qkv_kernel(normed_ref, w_ref, bias_ref, out_ref):
    out_ref[0, 0] = (nn(normed_ref[...], weight(w_ref)) + bias_ref[0, 0]).astype(BF)


def project_qkv(normed, gathered, bias):
    columns, width = gathered.shape[0], gathered.shape[-1]
    tokens = normed.shape[0]
    return pl.pallas_call(
        qkv_kernel,
        grid=(columns, 3),
        in_specs=[
            whole(normed),
            weight_spec(gathered, lambda y, c: (y, QKV + c)),
            pl.BlockSpec((1, 1, 1, width), lambda y, c: (y, c, 0, 0)),
        ],
        out_specs=pl.BlockSpec((1, 1, tokens, width), lambda y, c: (y, c, 0, 0)),
        out_shape=struct((columns, 3, tokens, width), BF),
        compiler_params=compiler_params(2),
        cost_estimate=cost(2 * tokens * D * 3 * columns * width, normed),
        name="project_qkv",
    )(normed, gathered, bias)


def head_row(head, value, lanes):
    lane = lax.broadcasted_iota(jnp.int32, (1, lanes), 1)
    inside = (lane >= head * HEAD_DIM) & (lane < (head + 1) * HEAD_DIM)
    return jnp.where(inside, value, 0.0).astype(BF)


def by_head(parts):
    lane = lax.broadcasted_iota(jnp.int32, (1, parts[0].shape[1]), 1)
    value = parts[0]
    for head in range(1, len(parts)):
        value = jnp.where(lane >= head * HEAD_DIM, parts[head], value)
    return value


def attend(query, key_rows, value_rows, bias, mixed_ref, weights_ref, inverse_ref):
    lanes = query.shape[1]
    heads = lanes // HEAD_DIM
    scores = []
    for head in range(heads):
        one = nt(query * head_row(head, HEAD_DIM**-0.5, lanes), key_rows)
        scores.append(one if bias is None else one + bias)
    mixed = []
    for head in range(heads):
        maximum = jnp.max(scores[head], axis=1, keepdims=True)
        weights = jnp.exp(scores[head] - maximum).astype(BF)
        weights_ref[0, 0, 0, head] = weights
        own = head_row(head, 1.0, lanes)
        mixed.append(nn(weights, value_rows * own + (1.0 - own.astype(F32)).astype(BF)))
    sums = by_head([mixed[(head - 1) % heads] for head in range(heads)])
    inverse = 1.0 / pltpu.roll(sums, lanes - HEAD_DIM, 1)
    inverse_ref[0] = inverse
    mixed_ref[0] = (by_head(mixed) * inverse).astype(BF)


def attend_back(query, key_rows, value_rows, mixed, grad_mixed, weights_ref, inverse):
    lanes = query.shape[1]
    heads = lanes // HEAD_DIM
    grad = (grad_mixed.astype(F32) * inverse).astype(BF)
    product = grad.astype(F32) * mixed.astype(F32)
    scaled = query * jnp.full((1, 1), HEAD_DIM**-0.5, BF)
    grad_weights = [nt(grad * head_row(head, 1.0, lanes), value_rows) for head in range(heads)]
    grad_query, grad_key, grad_value = [], [], []
    for head in range(heads):
        span = slice(head * HEAD_DIM, (head + 1) * HEAD_DIM)
        own = product * head_row(head, 1.0, lanes).astype(F32)
        inner = jnp.sum(own, axis=1, keepdims=True)
        weights = weights_ref[0, 0, 0, head]
        grad_value.append(tn(grad, weights)[span])
        grad_scores = (weights.astype(F32) * (grad_weights[head] - inner)).astype(BF)
        grad_query.append(nn(grad_scores, key_rows))
        grad_key.append(tn(scaled, grad_scores)[span])
    return (
        (by_head(grad_query) * HEAD_DIM**-0.5).astype(BF),
        jnp.concatenate(grad_key, axis=0).T.astype(BF),
        jnp.concatenate(grad_value, axis=0).T.astype(BF),
    )


def self_kernel(q_ref, k_ref, v_ref, row_ref, column_ref, mixed_ref, weights_ref, inverse_ref):
    bias = jnp.where(row_ref[0] <= column_ref[0], 0.0, NEGATIVE)
    attend(q_ref[0, 0], k_ref[0, 0], v_ref[0, 0], bias, mixed_ref, weights_ref, inverse_ref)


def attend_self(qkv, order_row, order_column):
    columns, _, tokens, width = qkv.shape
    seqs = order_row.shape[0]
    lanes = SELF_LANES if width % SELF_LANES == 0 else LANES
    groups, heads = width // lanes, lanes // HEAD_DIM

    def part(c):
        return pl.BlockSpec((1, 1, LEN, lanes), lambda y, p, s: (y, c, s, p))

    return pl.pallas_call(
        self_kernel,
        grid=(columns, groups, seqs),
        in_specs=[
            part(0),
            part(1),
            part(2),
            pl.BlockSpec((1, 1, LEN), lambda y, p, s: (s, 0, 0)),
            pl.BlockSpec((1, LEN, 1), lambda y, p, s: (s, 0, 0)),
        ],
        out_specs=[
            pl.BlockSpec((1, LEN, lanes), lambda y, p, s: (y, s, p)),
            pl.BlockSpec((1, 1, 1, heads, LEN, LEN), lambda y, p, s: (y, p, s, 0, 0, 0)),
            pl.BlockSpec((1, LEN, lanes), lambda y, p, s: (y, s, p)),
        ],
        out_shape=[
            struct((columns, tokens, width), BF),
            struct((columns, groups, seqs, heads, LEN, LEN), BF),
            struct((columns, tokens, width), F32),
        ],
        compiler_params=compiler_params(3),
        cost_estimate=cost(16 * columns * width * seqs * LEN * LEN, qkv),
        name="attend_self",
    )(qkv, qkv, qkv, order_row, order_column)


def out_kernel(mixed_ref, hidden_ref, vec_ref, wo_ref, wq_ref, bias_ref, first_ref, normed_ref, query_ref):
    step, columns = pl.program_id(0), pl.num_programs(0) // 2

    @pl.when(step == 0)
    def _():
        first_ref[...] = hidden_ref[...].astype(F32) + vec_ref[8:9, :]

    @pl.when(step < columns)
    def _():
        first_ref[...] += nt(mixed_ref[0], weight(wo_ref))

    @pl.when(step == columns - 1)
    def _():
        write_norm(first_ref, normed_ref, vec_ref[1:2, :], vec_ref[4:5, :])

    @pl.when(step >= columns)
    def _():
        query_ref[0] = (nn(normed_ref[...], weight(wq_ref)) + bias_ref[0]).astype(BF)


def project_out(mixed, hidden, vec, gathered, bias):
    columns, tokens, width = mixed.shape

    def early(i):
        return jnp.minimum(i, columns - 1)

    def late(i):
        return jnp.maximum(i - columns, 0)

    return pl.pallas_call(
        out_kernel,
        grid=(2 * columns,),
        in_specs=[
            pl.BlockSpec((1, tokens, width), lambda i: (early(i), 0, 0)),
            whole(hidden),
            whole(vec),
            weight_spec(gathered, lambda i: (early(i), OUT)),
            weight_spec(gathered, lambda i: (late(i), CQ)),
            pl.BlockSpec((1, 1, width), lambda i: (late(i), 0, 0)),
        ],
        out_specs=[
            whole(hidden),
            whole(hidden),
            pl.BlockSpec((1, tokens, width), lambda i: (late(i), 0, 0)),
        ],
        out_shape=[
            struct(hidden.shape, F32),
            struct(hidden.shape, BF),
            struct((columns, tokens, width), BF),
        ],
        compiler_params=compiler_params(1),
        cost_estimate=cost(4 * tokens * D * columns * width, hidden, hidden, mixed),
        name="project_out",
    )(mixed, hidden, vec, gathered, gathered, bias)


def pair_kernel(own_ref, frames_ref, w_ref, bias_ref, out_ref):
    out_ref[0, 0, 0] = (nn(frames_ref[0], weight(w_ref)) + bias_ref[0, 0]).astype(BF)


def project_pair(own, frames, gathered, bias, seqs):
    columns, width = gathered.shape[0], gathered.shape[-1]
    length = frames.shape[1]
    out = struct((columns, 2, seqs, length, width), BF)
    return pl.pallas_call(
        pair_kernel,
        grid_spec=pltpu.PrefetchScalarGridSpec(
            num_scalar_prefetch=1,
            grid=(seqs, columns, 2),
            in_specs=[
                pl.BlockSpec((1, length, D), lambda s, y, c, own: (s, 0, 0)),
                weight_spec(gathered, lambda s, y, c, own: (y, CKV + c)),
                pl.BlockSpec((1, 1, 1, width), lambda s, y, c, own: (y, c, 0, 0)),
            ],
            out_specs=pl.BlockSpec((1, 1, 1, length, width), lambda s, y, c, own: (y, c, s, 0, 0)),
        ),
        out_shape=out,
        compiler_params=compiler_params(3),
        cost_estimate=cost(4 * seqs * length * D * columns * width, out, out),
        name="project_pair",
    )(own, frames, gathered, bias)


def cross_kernel(q_ref, kv_ref, mixed_ref, weights_ref, inverse_ref):
    attend(q_ref[0], kv_ref[0, 0, 0], kv_ref[0, 1, 0], None, mixed_ref, weights_ref, inverse_ref)


def attend_cross(query, pair):
    columns, tokens, width = query.shape
    seqs, length, pairs = pair.shape[2], pair.shape[3], width // LANES
    return pl.pallas_call(
        cross_kernel,
        grid=(columns, pairs, seqs),
        in_specs=[
            pl.BlockSpec((1, LEN, LANES), lambda y, p, s: (y, s, p)),
            pl.BlockSpec((1, 2, 1, length, LANES), lambda y, p, s: (y, 0, s, 0, p)),
        ],
        out_specs=[
            pl.BlockSpec((1, LEN, LANES), lambda y, p, s: (y, s, p)),
            pl.BlockSpec((1, 1, 1, 2, LEN, length), lambda y, p, s: (y, p, s, 0, 0, 0)),
            pl.BlockSpec((1, LEN, LANES), lambda y, p, s: (y, s, p)),
        ],
        out_shape=[
            struct((columns, tokens, width), BF),
            struct((columns, pairs, seqs, 2, LEN, length), BF),
            struct((columns, tokens, width), F32),
        ],
        compiler_params=compiler_params(3),
        cost_estimate=cost(16 * columns * pairs * seqs * LEN * length * LANES, pair),
        name="attend_cross",
    )(query, pair)


def halves_of(value, own):
    width = value.shape[1] // 2
    low, high = value[:, :width], value[:, width:]
    return jnp.where(own == 0, high, low), jnp.where(own == 0, low, high)


def mlp_kernel(
    own_ref, mixed_ref, first_ref, vec_ref, wo_ref, wu_ref, wd_ref, bias_ref,
    second_ref, normed_ref, act_ref, slope_ref, send_ref, keep_ref, total_ref,
):
    step, columns = pl.program_id(0), 2

    @pl.when(step == 0)
    def _():
        second_ref[...] = first_ref[...] + vec_ref[11:12, :]

    @pl.when(step < columns)
    def _():
        second_ref[...] += nt(mixed_ref[0], weight(wo_ref))

    @pl.when(step == columns - 1)
    def _():
        write_norm(second_ref, normed_ref, vec_ref[2:3, :], vec_ref[5:6, :])
        total_ref[...] = second_ref[...] + vec_ref[12:13, :]

    @pl.when(step >= columns)
    def _():
        up, down = weight(wu_ref), weight(wd_ref)
        part = up.shape[1] // 2
        spans = [slice(p * part, (p + 1) * part) for p in range(2)]
        befores = [nn(normed_ref[...], up[:, span]) + bias_ref[0, 0, :, span] for span in spans]
        for span, before in zip(spans, befores):
            cdf = 0.5 + 0.5 * lax.erf(before * (0.5**0.5))
            density = jnp.exp(-0.5 * before * before) * (1.0 / math.sqrt(2.0 * math.pi))
            act = (before * cdf).astype(BF)
            act_ref[0, 0, :, span] = act
            slope_ref[0, 0, :, span] = (cdf + before * density).astype(BF)
            total_ref[...] += nt(act, down[:, span])

    @pl.when(step == pl.num_programs(0) - 1)
    def _():
        send, keep = halves_of(total_ref[...], own_ref[0])
        send_ref[...] = send.astype(BF)
        keep_ref[...] = keep.astype(BF)


def mlp_forward(own, mixed, first, vec, gathered, gathered_mlp, bias):
    columns, tokens, width = mixed.shape
    blocks = gathered_mlp.shape[2] // 2

    def early(i):
        return jnp.minimum(i, columns - 1)

    def late(i):
        rest = jnp.maximum(i - columns, 0)
        return rest // blocks, rest % blocks

    units = struct((columns, blocks, tokens, width), BF)
    half = struct((tokens, width), BF)
    unit_spec = pl.BlockSpec((1, 1, tokens, width), lambda i, own: (*late(i), 0, 0))
    return pl.pallas_call(
        mlp_kernel,
        grid_spec=pltpu.PrefetchScalarGridSpec(
            num_scalar_prefetch=1,
            grid=(columns + columns * blocks,),
            in_specs=[
                pl.BlockSpec((1, tokens, width), lambda i, own: (early(i), 0, 0)),
                whole(first),
                whole(vec),
                weight_spec(gathered, lambda i, own: (early(i), CO)),
                weight_spec(gathered_mlp, lambda i, own: late(i)),
                weight_spec(gathered_mlp, lambda i, own: (late(i)[0], blocks + late(i)[1])),
                pl.BlockSpec((1, 1, 1, width), lambda i, own: (*late(i), 0, 0)),
            ],
            out_specs=[whole(first), whole(first), unit_spec, unit_spec, whole(half), whole(half)],
            scratch_shapes=[pltpu.VMEM(first.shape, F32)],
        ),
        out_shape=[struct(first.shape, F32), struct(first.shape, BF), units, units, half, half],
        compiler_params=compiler_params(1),
        cost_estimate=cost(tokens * D * columns * width * (2 + 4 * blocks), first, units, units, gathered_mlp),
        name="mlp_forward",
    )(own, mixed, first, vec, gathered, gathered_mlp, gathered_mlp, bias)


def mlp_back_kernel(
    grad_ref, second_ref, vec_ref, wd_ref, wu_ref, wo_ref, slope_ref,
    before_ref, unit_sum_ref, grad_second_ref, low_ref, sums_ref, mixed_ref, total_ref,
):
    step, columns = pl.program_id(0), mixed_ref.shape[1] * 0 + vec_ref.shape[1] // mixed_ref.shape[2]
    last = pl.num_programs(0) - columns

    @pl.when(step == 0)
    def _():
        total_ref[...] = jnp.zeros_like(total_ref)

    @pl.when(step < last)
    def _():
        grad_act = nn(grad_ref[...], weight(wd_ref))
        before = (grad_act * slope_ref[0, 0].astype(F32)).astype(BF)
        before_ref[0, 0] = before
        unit_sum_ref[0, 0] = jnp.sum(before.astype(F32), axis=0, keepdims=True)
        total_ref[...] += nt(before, weight(wu_ref))

    @pl.when(step == last - 1)
    def _():
        def finish(rows, back):
            incoming = grad_ref[rows, :].astype(F32)
            value = incoming + back
            grad_second_ref[rows, :] = value
            low_ref[rows, :] = value.astype(BF)
            return value.astype(BF)

        write_norm_back(total_ref, second_ref, vec_ref[2:3, :], sums_ref, finish)
        sums_ref[3:4, :] = jnp.sum(grad_ref[...].astype(F32), axis=0, keepdims=True)

    @pl.when(step >= last)
    def _():
        mixed_ref[0] = nn(low_ref[...], weight(wo_ref)).astype(BF)


def mlp_backward(grad, second, vec, gathered, gathered_mlp, slope):
    columns, blocks, tokens, width = slope.shape

    def early(i):
        rest = jnp.minimum(i, columns * blocks - 1)
        return rest // blocks, rest % blocks

    def late(i):
        return jnp.maximum(i - columns * blocks, 0)

    unit_spec = pl.BlockSpec((1, 1, tokens, width), lambda i: (*early(i), 0, 0))
    sums = struct((8, D), F32)
    return pl.pallas_call(
        mlp_back_kernel,
        grid=(columns * blocks + columns,),
        in_specs=[
            whole(grad),
            whole(second),
            whole(vec),
            weight_spec(gathered_mlp, lambda i: (early(i)[0], blocks + early(i)[1])),
            weight_spec(gathered_mlp, lambda i: early(i)),
            weight_spec(gathered, lambda i: (late(i), CO)),
            unit_spec,
        ],
        out_specs=[
            unit_spec,
            pl.BlockSpec((1, 1, 1, width), lambda i: (*early(i), 0, 0)),
            whole(second),
            whole(grad),
            whole(sums),
            pl.BlockSpec((1, tokens, width), lambda i: (late(i), 0, 0)),
        ],
        out_shape=[
            struct(slope.shape, BF),
            struct((columns, blocks, 1, width), F32),
            struct(second.shape, F32),
            struct(grad.shape, BF),
            sums,
            struct((columns, tokens, width), BF),
        ],
        scratch_shapes=[pltpu.VMEM(second.shape, F32)],
        compiler_params=compiler_params(1),
        cost_estimate=cost(tokens * D * columns * width * (2 + 4 * blocks), second, slope, slope, gathered_mlp),
        name="mlp_backward",
    )(grad, second, vec, gathered_mlp, gathered_mlp, gathered, slope)


def cross_back_kernel(
    q_ref, kv_ref, mixed_ref, grad_ref, weights_ref, inverse_ref, query_ref, pair_ref, sums_ref
):
    grad_query, grad_key, grad_value = attend_back(
        q_ref[0], kv_ref[0, 0, 0], kv_ref[0, 1, 0], mixed_ref[0], grad_ref[0], weights_ref, inverse_ref[0]
    )
    query_ref[0] = grad_query
    pair_ref[0, 0, 0] = grad_key
    pair_ref[0, 1, 0] = grad_value

    @pl.when(pl.program_id(2) == 0)
    def _():
        sums_ref[...] = jnp.zeros_like(sums_ref)

    sums_ref[0, 0:1, :] += jnp.sum(grad_query.astype(F32), axis=0, keepdims=True)
    sums_ref[0, 1:2, :] += jnp.sum(grad_value.astype(F32), axis=0, keepdims=True)


def attend_cross_back(query, pair, mixed, grad, weights, inverse):
    columns, tokens, width = query.shape
    seqs, length, pairs = pair.shape[2], pair.shape[3], width // LANES
    row_spec = pl.BlockSpec((1, LEN, LANES), lambda y, p, s: (y, s, p))
    pair_spec = pl.BlockSpec((1, 2, 1, length, LANES), lambda y, p, s: (y, 0, s, 0, p))
    return pl.pallas_call(
        cross_back_kernel,
        grid=(columns, pairs, seqs),
        in_specs=[
            row_spec,
            pair_spec,
            row_spec,
            row_spec,
            pl.BlockSpec((1, 1, 1, 2, LEN, length), lambda y, p, s: (y, p, s, 0, 0, 0)),
            row_spec,
        ],
        out_specs=[row_spec, pair_spec, pl.BlockSpec((1, 8, LANES), lambda y, p, s: (y, 0, p))],
        out_shape=[
            struct(query.shape, BF),
            struct(pair.shape, BF),
            struct((columns, 8, width), F32),
        ],
        compiler_params=compiler_params(3),
        cost_estimate=cost(32 * columns * pairs * seqs * LEN * length * LANES, pair, pair),
        name="attend_cross_back",
    )(query, pair, mixed, grad, weights, inverse)


def self_back_kernel(
    q_ref, k_ref, v_ref, mixed_ref, grad_ref, weights_ref, inverse_ref, out_ref, sums_ref
):
    grad_query, grad_key, grad_value = attend_back(
        q_ref[0, 0], k_ref[0, 0], v_ref[0, 0], mixed_ref[0], grad_ref[0], weights_ref, inverse_ref[0]
    )
    out_ref[0, 0] = grad_query
    out_ref[0, 1] = grad_key
    out_ref[0, 2] = grad_value

    @pl.when(pl.program_id(2) == 0)
    def _():
        sums_ref[...] = jnp.zeros_like(sums_ref)

    sums_ref[0, 0:1, :] += jnp.sum(grad_query.astype(F32), axis=0, keepdims=True)
    sums_ref[0, 1:2, :] += jnp.sum(grad_value.astype(F32), axis=0, keepdims=True)


def attend_self_back(qkv, mixed, grad, weights, inverse):
    columns, _, tokens, width = qkv.shape
    groups, seqs, heads = weights.shape[1:4]
    lanes = heads * HEAD_DIM
    row_spec = pl.BlockSpec((1, LEN, lanes), lambda y, p, s: (y, s, p))

    def part(c):
        return pl.BlockSpec((1, 1, LEN, lanes), lambda y, p, s: (y, c, s, p))

    return pl.pallas_call(
        self_back_kernel,
        grid=(columns, groups, seqs),
        in_specs=[
            part(0),
            part(1),
            part(2),
            row_spec,
            row_spec,
            pl.BlockSpec((1, 1, 1, heads, LEN, LEN), lambda y, p, s: (y, p, s, 0, 0, 0)),
            row_spec,
        ],
        out_specs=[
            pl.BlockSpec((1, 3, LEN, lanes), lambda y, p, s: (y, 0, s, p)),
            pl.BlockSpec((1, 8, lanes), lambda y, p, s: (y, 0, p)),
        ],
        out_shape=[struct(qkv.shape, BF), struct((columns, 8, width), F32)],
        compiler_params=compiler_params(3),
        cost_estimate=cost(32 * columns * width * seqs * LEN * LEN, qkv, qkv),
        name="attend_self_back",
    )(qkv, qkv, qkv, mixed, grad, weights, inverse)


def query_back_kernel(
    grad_ref, first_ref, second_ref, vec_ref, wq_ref, wo_ref,
    grad_first_ref, low_ref, sums_ref, mixed_ref, total_ref,
):
    step, columns = pl.program_id(0), pl.num_programs(0) // 2

    @pl.when(step == 0)
    def _():
        total_ref[...] = jnp.zeros_like(total_ref)

    @pl.when(step < columns)
    def _():
        total_ref[...] += nt(grad_ref[0], weight(wq_ref))

    @pl.when(step == columns - 1)
    def _():
        def finish(rows, back):
            value = second_ref[rows, :] + back
            grad_first_ref[rows, :] = value
            low_ref[rows, :] = value.astype(BF)
            return value.astype(BF)

        write_norm_back(total_ref, first_ref, vec_ref[1:2, :], sums_ref, finish)

    @pl.when(step >= columns)
    def _():
        mixed_ref[0] = nn(low_ref[...], weight(wo_ref)).astype(BF)


def query_backward(grad, first, grad_second, vec, gathered):
    columns, tokens, width = grad.shape

    def early(i):
        return jnp.minimum(i, columns - 1)

    def late(i):
        return jnp.maximum(i - columns, 0)

    sums = struct((8, D), F32)
    return pl.pallas_call(
        query_back_kernel,
        grid=(2 * columns,),
        in_specs=[
            pl.BlockSpec((1, tokens, width), lambda i: (early(i), 0, 0)),
            whole(first),
            whole(first),
            whole(vec),
            weight_spec(gathered, lambda i: (early(i), CQ)),
            weight_spec(gathered, lambda i: (late(i), OUT)),
        ],
        out_specs=[
            whole(first),
            whole(first),
            whole(sums),
            pl.BlockSpec((1, tokens, width), lambda i: (late(i), 0, 0)),
        ],
        out_shape=[struct(first.shape, F32), struct(first.shape, BF), sums, struct(grad.shape, BF)],
        scratch_shapes=[pltpu.VMEM(first.shape, F32)],
        compiler_params=compiler_params(1),
        cost_estimate=cost(4 * tokens * D * columns * width, first, first, first, grad),
        name="query_backward",
    )(grad, first, grad_second, vec, gathered, gathered)


def hidden_back_kernel(
    own_ref, grad_ref, hidden_ref, first_ref, vec_ref, w_ref, send_ref, keep_ref, sums_ref, total_ref
):
    part = total_ref.shape[1] // 2
    product = nt(joined(grad_ref), weight_rows(w_ref))
    for half in range(2):

        @pl.when(pl.program_id(0) == half)
        def _():
            total_ref[:, half * part : (half + 1) * part] = product

    @pl.when(pl.program_id(0) == 1)
    def _():
        def finish(rows, back):
            value = first_ref[rows, :] + back
            send, keep = halves_of(value, own_ref[0])
            send_ref[rows, :] = send.astype(BF)
            keep_ref[rows, :] = keep
            return value

        write_norm_back(total_ref, hidden_ref, vec_ref[0:1, :], sums_ref, finish)


def hidden_backward(own, grad, hidden, grad_first, vec, gathered):
    columns, _, tokens, width = grad.shape
    _, shards, _, rows, _ = gathered.shape
    sums, half = struct((8, D), F32), struct((tokens, width), F32)
    return pl.pallas_call(
        hidden_back_kernel,
        grid_spec=pltpu.PrefetchScalarGridSpec(
            num_scalar_prefetch=1,
            grid=(2,),
            in_specs=[
                whole(grad),
                whole(hidden),
                whole(grad_first),
                whole(vec),
                pl.BlockSpec((columns, shards // 2, 3, rows, width), lambda i, own: (0, i, QKV, 0, 0)),
            ],
            out_specs=[whole(half), whole(half), whole(sums)],
            scratch_shapes=[pltpu.VMEM(hidden.shape, F32)],
        ),
        out_shape=[struct((tokens, width), BF), half, sums],
        compiler_params=compiler_params(1),
        cost_estimate=cost(6 * tokens * D * columns * width, grad, grad_first, hidden, grad_first),
        name="hidden_backward",
    )(own, grad, hidden, grad_first, vec, gathered)


def joined(ref):
    return jnp.concatenate([ref[y, c] for y in range(ref.shape[0]) for c in range(ref.shape[1])], axis=1)


def weight_rows(ref):
    columns, shards, blocks, rows, width = ref.shape
    parts = [ref[y, :, c].reshape(shards * rows, width) for y in range(columns) for c in range(blocks)]
    return jnp.concatenate(parts, axis=1)


def frames_back_kernel(own_ref, grad_ref, w_ref, send_ref, keep_ref):
    grad = jnp.concatenate([grad_ref[y, c, 0] for y in range(grad_ref.shape[0]) for c in range(2)], axis=1)
    value = nt(grad, weight_rows(w_ref)).astype(BF)
    length, width = value.shape
    for part, ref in ((0, send_ref), (1, keep_ref)):

        @pl.when(pl.program_id(1) == part)
        def _():
            ref[0, :length] = value
            ref[0, length:] = jnp.zeros((ref.shape[1] - length, width), BF)


def frames_backward(own, grad, gathered):
    columns, _, seqs, length, width = grad.shape
    _, shards, _, rows, _ = gathered.shape
    padded = -(-length // 32) * 32
    half = struct((seqs, padded, width), BF)
    half_spec = pl.BlockSpec((1, padded, width), lambda s, i, own: (s, 0, 0))
    return pl.pallas_call(
        frames_back_kernel,
        grid_spec=pltpu.PrefetchScalarGridSpec(
            num_scalar_prefetch=1,
            grid=(seqs, 2),
            in_specs=[
                pl.BlockSpec((columns, 2, 1, length, width), lambda s, i, own: (0, 0, s, 0, 0)),
                pl.BlockSpec(
                    (columns, shards // 2, 2, rows, width),
                    lambda s, i, own: (0, jnp.where(i == 1, own[0], 1 - own[0]), CKV // 2, 0, 0),
                ),
            ],
            out_specs=[half_spec, half_spec],
        ),
        out_shape=[half, half],
        compiler_params=compiler_params(2),
        cost_estimate=cost(4 * seqs * length * D * columns * width, grad, grad),
        name="frames_backward",
    )(own, grad, gathered)


class Plan:
    def __init__(self, order, bits):
        self.order, self.rest, self.bits = order, 1 << (bits - 2), bits
        self.sizes = {"x": 2, "y": 2, "z": self.rest}
        self.cuts = tuple(self.sizes[c] for c in order)

    def block(self, step_index):
        return tuple(1 if c == "y" else self.sizes[c] for c in self.order)

    def place(self, column):
        return tuple(column if c == "y" else 0 for c in self.order)

    def store(self, ref, value):
        rows = value.shape[0] // (2 * self.rest)
        value = value.reshape(2, self.rest, rows, value.shape[1])
        if self.order.index("x") > self.order.index("z"):
            value = value.swapaxes(0, 1)
        at = tuple(0 if c == "y" else slice(None) for c in self.order)
        ref[at + (0,)] = value


def cut_rows(place_ref, source, turned_ref, shards):
    rows = source.shape[0] // shards
    for shard in range(shards):
        at = pl.multiple_of(place_ref[1 + shard] * rows, rows)
        turned_ref[pl.ds(at, rows), :] = source[shard * rows : (shard + 1) * rows]


def turn_kernel(bits, place_ref, source_ref, turned_ref):
    cut_rows(place_ref, source_ref[0].T, turned_ref.at[0], 1 << bits)


def turn(bits, place, source):
    seqs, tokens, depth = source.shape
    return pl.pallas_call(
        functools.partial(turn_kernel, bits),
        grid_spec=pltpu.PrefetchScalarGridSpec(
            num_scalar_prefetch=1,
            grid=(seqs,),
            in_specs=[pl.BlockSpec((1, tokens, depth), lambda s, place: (s, 0, 0))],
            out_specs=pl.BlockSpec((1, depth, tokens), lambda s, place: (s, 0, 0)),
        ),
        out_shape=struct((seqs, depth, tokens), BF),
        compiler_params=compiler_params(1),
        cost_estimate=cost(0, source),
        name="turn",
    )(place, source)


def weight_kernel(plan, turned, place_ref, left_ref, right_ref, *refs):
    if turned:
        send_ref, keep_ref = refs[-2:]
        lefts = [left_ref[s] for s in range(left_ref.shape[0])]
    else:
        send_ref, keep_ref, turned_ref = refs[-3:]

        @pl.when((pl.program_id(0) == 0) & (pl.program_id(1) == 0))
        def _():
            cut_rows(place_ref, left_ref[...].T, turned_ref, 1 << plan.bits)

        lefts = [turned_ref[...]]
    total = 0.0
    for s, left in enumerate(lefts):
        total = total + nn(left, right_ref[0, 0, s])
    half = total.shape[0] // 2
    plan.store(send_ref, total[:half].astype(BF))
    plan.store(keep_ref, total[half:].astype(BF))


def weight_grad(plan, place, left, right, first=0, count=None, at=0, room=None, into=()):
    columns, blocks, seqs, tokens, width = right.shape
    blocks = count or blocks
    rows = D >> plan.bits
    turned = len(left.shape) == 3
    part = struct(plan.cuts + (room or blocks, rows, width), BF)
    out_spec = pl.BlockSpec(
        plan.block(0) + (1, rows, width),
        lambda y, i, place: plan.place(y) + (at + i, 0, 0),
    )

    def right_index(y, i, place):
        return (jnp.where(y == 1, place[0], 1 - place[0]), first + i, 0, 0, 0)

    return pl.pallas_call(
        functools.partial(weight_kernel, plan, turned),
        grid_spec=pltpu.PrefetchScalarGridSpec(
            num_scalar_prefetch=1,
            grid=(columns, blocks),
            in_specs=[whole(left), pl.BlockSpec((1, 1, seqs, tokens, width), right_index)]
            + [pl.BlockSpec(memory_space=pl.ANY) for _ in into],
            out_specs=[out_spec, out_spec],
            scratch_shapes=[] if turned else [pltpu.VMEM((D, tokens), BF)],
        ),
        out_shape=[part, part],
        input_output_aliases={3: 0, 4: 1} if into else {},
        compiler_params=compiler_params(2),
        cost_estimate=cost(2 * columns * blocks * seqs * tokens * width * D, right, part, part),
        name="weight_grad",
    )(place, left, right, *into)


def cut_kernel(starts, *refs):
    step, count = pl.program_id(0), len(starts) - 1
    for p in range(count):
        keep_ref, got_ref = refs[2 * p], refs[2 * p + 1]
        outs = refs[2 * (count + p)], refs[2 * (count + p) + 1]

        @pl.when((step >= starts[p]) & (step < starts[p + 1]))
        def _():
            for part in (0, 1):
                outs[part][...] = keep_ref[part] + got_ref[part]


def add_and_cut(pairs):
    starts, arrays, in_specs, out_specs, outs = [0], [], [], [], []
    for keep, got in pairs:
        width = keep.shape[-1]
        rows = math.prod(keep.shape[1:-1])
        block = math.gcd(rows, 512)
        begin, blocks = starts[-1], rows // block
        starts.append(begin + blocks)

        def index(i, begin=begin, blocks=blocks):
            return jnp.clip(i - begin, 0, blocks - 1)

        arrays += [keep.reshape(2, rows, width), got.reshape(2, rows, width)]
        in_specs += [pl.BlockSpec((2, block, width), lambda i, index=index: (0, index(i), 0))] * 2
        out_specs += [pl.BlockSpec((block, width), lambda i, index=index: (index(i), 0))] * 2
        outs += [struct((rows, width), BF)] * 2
    results = pl.pallas_call(
        functools.partial(cut_kernel, tuple(starts)),
        grid=(starts[-1],),
        in_specs=in_specs,
        out_specs=out_specs,
        out_shape=outs,
        compiler_params=compiler_params(1),
        cost_estimate=cost(0, *arrays),
        name="add_and_cut",
    )(*arrays)
    return [
        tuple(r.reshape(keep.shape[1:]) for r in results[2 * p : 2 * p + 2])
        for p, (keep, _) in enumerate(pairs)
    ]


def frames_join_kernel(own_ref, keep_ref, *refs):
    *got_refs, out_ref = refs
    length, seqs = out_ref.shape[0], keep_ref.shape[0]
    for s in range(seqs):
        keep = keep_ref[s, :length].astype(F32)
        got = jnp.concatenate([got_refs[2 * s][0], got_refs[2 * s + 1][0]], axis=0)[:length].astype(F32)
        out_ref[:, s, :] = jnp.where(own_ref[0] == 0, keep, got)
        out_ref[:, seqs + s, :] = jnp.where(own_ref[0] == 0, got, keep)


def join_frames(own, keep, *arguments):
    *got, length = arguments
    seqs, padded, width = keep.shape
    return pl.pallas_call(
        frames_join_kernel,
        grid_spec=pltpu.PrefetchScalarGridSpec(
            num_scalar_prefetch=1,
            grid=(width // LANES,),
            in_specs=[pl.BlockSpec((seqs, padded, LANES), lambda i, own: (0, 0, i))]
            + [pl.BlockSpec((1, padded // 2, LANES), lambda i, own: (0, 0, i))] * (2 * seqs),
            out_specs=pl.BlockSpec((length, 2 * seqs, LANES), lambda i, own: (0, 0, i)),
        ),
        out_shape=struct((length, 2 * seqs, width), F32),
        compiler_params=compiler_params(1),
        cost_estimate=cost(0, keep),
        name="join_frames",
    )(own, keep, *got)


def swap(axis, bit, value):
    size = lax.axis_size(axis)
    return lax.ppermute(value, axis, [(d, d ^ (1 << bit)) for d in range(size)])


def pick(array, index, axis):
    return lax.dynamic_index_in_dim(array, index, axis, keepdims=False)


def exchange(keep, send):
    if lax.axis_size("tp") != 2:
        got = lax.all_to_all(send, "tp", split_axis=0, concat_axis=0, tiled=True)
        return got.astype(keep.dtype)
    own = lax.axis_index("tp")
    got = swap("tp", 0, pick(send, 1 - own, 0)).astype(keep.dtype)
    mine = pick(keep, own, 0)
    return jnp.where(own == 0, jnp.stack([mine, got]), jnp.stack([got, mine]))


def bits_of(axis):
    return lax.axis_size(axis).bit_length() - 1


class Chain:
    def __init__(self):
        self.token = None

    def tie(self, *values):
        if self.token is None:
            return values
        return lax.optimization_barrier((*values, self.token))[:-1]

    def hold(self, value):
        (self.token,) = self.tie(value)
        return self.token


class Reduction:
    def __init__(self, plan, parts):
        self.result, self.got = None, None
        stages = {"x": [("dp", 1)], "y": [("tp", 0)], "z": [("dp", b) for b in range(2, plan.bits)]}
        self.order = [("dp", 0)] + [stage for c in plan.order for stage in stages[c]]
        cuts = []
        for c in plan.order:
            cuts += [2] * len(stages[c])
        self.send, self.keep = (p.reshape(tuple(cuts) + p.shape[len(plan.cuts) :]) for p in parts)


def launch(chain, reductions):
    for one in reductions:
        one.got = swap(*one.order.pop(0), chain.tie(one.send)[0])


def advance(chain, *reductions):
    open_ones = [one for one in reductions if one.got is not None and one.order]
    if open_ones:
        tied = chain.tie(*[a for one in open_ones for a in (one.keep, one.got)])
        pieces = add_and_cut([tied[2 * i : 2 * i + 2] for i in range(len(open_ones))])
        for one, (send, keep) in zip(open_ones, pieces):
            one.send, one.keep = send, keep
        chain.token = pieces[-1][0]
    launch(chain, [one for one in reductions if one.order])


def finish(chain, *reductions):
    while any(one.order for one in reductions):
        advance(chain, *[one for one in reductions if one.order])
    return [one.keep.astype(F32) + one.got.astype(F32) for one in reductions]


def per_device_whole_sequences(
    hidden_in, encoder_states, positions, self_qkv, self_out, cross_query, cross_kv, cross_out,
    up_weight, down_weight, norm_gains, bias_rows, up_bias, out_grad,
):
    columns, shards = lax.axis_size("tp"), lax.axis_size("dp")
    own = lax.axis_index("tp")
    width = hidden_in.shape[1]
    tokens = hidden_in.shape[0] // columns
    seqs = positions.shape[0] // columns
    own_index = own.astype(jnp.int32).reshape(1)

    attention_part = jnp.concatenate(
        [
            self_qkv.transpose(1, 0, 2),
            self_out.T[None],
            cross_kv.transpose(1, 0, 2),
            cross_query[None],
            cross_out.T[None],
        ]
    )
    rows = up_weight.shape[0]
    blocks = up_weight.shape[1] // width
    mlp_part = jnp.concatenate(
        [
            up_weight.reshape(rows, blocks, width).transpose(1, 0, 2),
            down_weight.reshape(blocks, width, rows).transpose(0, 2, 1),
        ]
    )

    def gather(part):
        full = lax.all_gather(part, ("tp", "dp"), axis=0)
        return full.reshape((columns, shards) + part.shape)

    weights, weights_mlp = gather(attention_part), gather(mlp_part)

    def to_tokens(array):
        mine = lax.dynamic_slice_in_dim(array, own * tokens, tokens, 0)
        got = swap("tp", 0, lax.dynamic_slice_in_dim(array, (1 - own) * tokens, tokens, 0))
        return jnp.where(
            own == 0, jnp.concatenate([mine, got], axis=1), jnp.concatenate([got, mine], axis=1)
        )

    hidden = lax.optimization_barrier(to_tokens(hidden_in))
    grad_final = lax.optimization_barrier(to_tokens(out_grad))
    small = jnp.concatenate([norm_gains, bias_rows, up_bias.reshape(blocks, width)])
    every = jnp.broadcast_to(small, (columns,) + small.shape)
    every = exchange(every, every)
    vec = every[:, :13].transpose(1, 0, 2).reshape(13, columns * width)
    vec = jnp.concatenate([vec, jnp.zeros((3, columns * width), F32)])
    none = jnp.zeros((columns, width), F32)
    bias = lambda row: every[:, 3 + row]
    qkv_bias = jnp.stack([bias(3), none, bias(4)], axis=1)[:, :, None]
    pair_bias = jnp.stack([none, bias(7)], axis=1)[:, :, None]
    up_rows = every[:, 13:][:, :, None]
    order = lax.dynamic_slice_in_dim(positions, own * seqs, seqs, 0)

    frames = lax.optimization_barrier(
        lax.dynamic_slice_in_dim(encoder_states, own * seqs, seqs, 0)
    )

    bits = bits_of("dp")
    device = lax.axis_index("dp")
    shard = jnp.arange(shards)
    same = ~(shard ^ device)
    spot = sum(((same >> b) & 1) << (bits - 1 - b) for b in range(bits))
    place = jnp.concatenate([own_index, spot.astype(jnp.int32)])
    turned_frames = turn(bits, place, frames)
    turned_grad = turn(bits, place, grad_final[None])

    normed_a = first_norm(hidden, vec)
    turned_a = turn(bits, place, normed_a[None])
    ready = lax.optimization_barrier((normed_a, turned_a, turned_frames, turned_grad))
    qkv = project_qkv(ready[0], weights, qkv_bias)
    pair = project_pair(own_index, frames, weights, pair_bias, seqs)
    mixed_a, *attention_a = attend_self(qkv, order[:, None, :], order[:, :, None])
    first, normed_c, query = project_out(mixed_a, hidden, vec, weights, bias(6)[:, None])
    mixed_c, *attention_c = attend_cross(query, pair)
    turned_c = turn(bits, place, normed_c[None])
    mixed_now, _ = lax.optimization_barrier((mixed_c, turned_c))
    second, normed_m, activated, slope, send_output, keep_output = mlp_forward(
        own_index, mixed_now, first, vec, weights, weights_mlp, up_rows
    )

    got_output = swap("tp", 0, send_output)

    def pair_up(keep, got):
        got = got.astype(keep.dtype)
        return jnp.where(own == 0, jnp.stack([keep, got]), jnp.stack([got, keep]))

    chain = Chain()
    chain.token = send_output

    def gradient(order, left, right, **options):
        parts = weight_grad(Plan(order, bits), place, left, chain.tie(right)[0], **options)
        chain.token = parts[0]
        return parts

    def reduction(order, left, right, **options):
        return Reduction(Plan(order, bits), gradient(order, left, right, **options))

    def run(kernel, first_array, *arrays):
        (first_array,) = chain.tie(first_array)
        results = kernel(first_array, *arrays)
        chain.token = results[0]
        return results

    down = reduction("xyz", turned_grad, activated[:, :, None])
    advance(chain, down)
    grad_before, up_sums, grad_second, low_second, sums_m, grad_mixed_c = run(
        mlp_backward, grad_final, second, vec, weights, weights_mlp, slope
    )
    output = pair_up(keep_output, chain.hold(got_output)).reshape(columns * tokens, width)
    advance(chain, down)
    up = reduction("yxz", normed_m, grad_before[:, :, None])
    advance(chain, up)
    two = gradient("zxy", low_second, mixed_c[:, None, None], room=2)
    advance(chain, up)
    (grad_mixed_c,) = chain.tie(grad_mixed_c)
    grad_query, grad_pair, sums_cross = run(attend_cross_back, query, pair, mixed_c, grad_mixed_c, *attention_c)
    advance(chain, down, up)
    send_frames, keep_frames = run(
        lambda grad: frames_backward(own_index, grad, weights), grad_pair
    )
    advance(chain, down, up)
    parts = chain.tie(send_frames)[0].reshape(2 * seqs, -1, width)
    got_frames = [swap("tp", 0, part) for part in jnp.split(parts, 2 * seqs)]
    kv = reduction("xyz", turned_frames, grad_pair)
    two = reduction("zxy", turned_c, grad_query[:, None, None], at=1, room=2, into=two)
    got_frames[:seqs] = [chain.hold(part) for part in got_frames[:seqs]]
    advance(chain, down, up, kv, two)
    grad_first, low_first, sums_c, grad_mixed_a = run(
        query_backward, grad_query, first, grad_second, vec, weights
    )
    last = gradient("xyz", low_first, mixed_a[:, None, None], room=2)
    got_frames[seqs] = chain.hold(got_frames[seqs])
    advance(chain, kv, two)
    (grad_mixed_a,) = chain.tie(grad_mixed_a)
    grad_triple, sums_self = run(attend_self_back, qkv, mixed_a, grad_mixed_a, *attention_a)
    got_frames[seqs + 1 :] = [chain.hold(part) for part in got_frames[seqs + 1 :]]
    advance(chain, kv, two)
    pairs = reduction("yxz", turned_a, grad_triple[:, :, None], first=1, count=2)
    advance(chain, pairs)
    last = reduction("xyz", turned_a, grad_triple[:, :, None], count=1, at=1, room=2, into=last)
    advance(chain, last)
    advance(chain, pairs, last)
    send_hidden, keep_hidden, sums_a = run(
        lambda grad: hidden_backward(own_index, grad, hidden, grad_first, vec, weights), grad_triple
    )
    advance(chain, kv, two, pairs, last)
    got_hidden = swap("tp", 0, chain.tie(send_hidden)[0])

    halves = lambda row: row.reshape(columns, width)
    gains = [halves(sums[0]) for sums in (sums_a, sums_c, sums_m)]
    shifts = [halves(sums[1]) for sums in (sums_a, sums_c, sums_m)]
    sums = jnp.stack(
        gains
        + shifts
        + [
            sums_self[:, 0],
            sums_self[:, 1],
            halves(sums_c[2]),
            sums_cross[:, 0],
            sums_cross[:, 1],
            halves(sums_m[2]),
            halves(sums_m[3]),
        ],
        axis=1,
    )
    totals = jnp.concatenate([sums, up_sums[:, :, 0]], axis=1)
    def spread(totals, bit):
        return totals + chain.hold(swap("dp", bit, totals))

    totals = spread(totals, 0)
    (keep_frames,) = chain.tie(keep_frames)
    encoder_grad = join_frames(own_index, keep_frames, *got_frames, frames.shape[1])
    chain.token = encoder_grad
    advance(chain, kv, two, pairs, last)
    totals = spread(totals, 1)
    hidden_grad = pair_up(keep_hidden, chain.hold(got_hidden)).reshape(columns * tokens, width)
    hidden_grad = chain.hold(hidden_grad)
    advance(chain, pairs, last)
    for bit in range(2, bits):
        totals = spread(totals, bit)
    totals = pick(totals, own, 0) + swap("tp", 0, pick(totals, 1 - own, 0))
    encoder_grad = encoder_grad.transpose(1, 0, 2)
    own_down, own_up, own_kv, own_two, own_pairs, own_last = finish(chain, down, up, kv, two, pairs, last)
    own_qkv = jnp.concatenate([own_last[1:], own_pairs])

    return (
        output,
        hidden_grad,
        encoder_grad,
        own_qkv.transpose(1, 0, 2),
        own_last[0].T,
        own_two[1],
        own_kv.transpose(1, 0, 2),
        own_two[0].T,
        own_up.transpose(1, 0, 2).reshape(rows, blocks * width),
        own_down.transpose(0, 2, 1).reshape(blocks * width, rows),
        totals[:3],
        totals[3:13],
        totals[13:].reshape(blocks * width),
    )


def to_heads(matrix, groups):
    return matrix.reshape(groups, -1, matrix.shape[-1] // HEAD_DIM, HEAD_DIM)


def norm_forward(values, gain, shift):
    row_sum, square_sum = lax.psum(
        (jnp.sum(values, axis=1), jnp.sum(values * values, axis=1)), "tp"
    )
    width = values.shape[1] * lax.axis_size("tp")
    row_mean = row_sum / width
    inverse = lax.rsqrt(square_sum / width - row_mean * row_mean + EPSILON)
    unit = (values - row_mean[:, None]) * inverse[:, None]
    normed = (unit * gain + shift).astype(jnp.bfloat16)
    return (lax.all_gather(normed, "tp", axis=1, tiled=True), unit, inverse)


def norm_backward(incoming, unit, inverse, gain):
    scaled = incoming * gain
    first_sum, second_sum = lax.psum(
        (jnp.sum(scaled, axis=1), jnp.sum(scaled * unit, axis=1)), "tp"
    )
    width = incoming.shape[1] * lax.axis_size("tp")
    outgoing = inverse[:, None] * (
        scaled - first_sum[:, None] / width - unit * (second_sum[:, None] / width)
    )
    return (outgoing, jnp.sum(incoming * unit, axis=0), jnp.sum(incoming, axis=0))


def branch_total(partial_value):
    return lax.psum_scatter(partial_value, "tp", scatter_dimension=1, tiled=True)


def spread_grad(incoming):
    return lax.all_gather(incoming.astype(jnp.bfloat16), "tp", axis=1, tiled=True)


def spread_heads(columns):
    return lax.all_gather(columns, "tp", axis=1, tiled=True)


def input_total(partial_value):
    return lax.psum_scatter(partial_value, "tp", scatter_dimension=1, tiled=True)


def scores_of(query, key_rows, visible):
    scores = jnp.einsum(
        "sqhe,skhe->shqk", query, key_rows, preferred_element_type=jnp.float32
    ) * HEAD_DIM ** (-0.5)
    if visible is None:
        return scores
    return jnp.where(visible[:, None], scores, NEGATIVE)


def attend_forward(query, key_rows, value_rows, visible):
    scores = scores_of(query, key_rows, visible)
    row_max = jnp.max(scores, axis=-1, keepdims=True)
    weights = jnp.exp(scores - row_max)
    row_total = jnp.sum(weights, axis=-1, keepdims=True)
    probs = (weights / row_total).astype(jnp.bfloat16)
    mixed = jnp.einsum("shqk,skhe->sqhe", probs, value_rows, preferred_element_type=jnp.float32)
    return (mixed.astype(jnp.bfloat16), row_max + jnp.log(row_total))


def attend_backward(query, key_rows, value_rows, visible, log_total, grad_mixed):
    weights = jnp.exp(scores_of(query, key_rows, visible) - log_total)
    grad_weights = jnp.einsum(
        "sqhe,skhe->shqk", grad_mixed, value_rows, preferred_element_type=jnp.float32
    )
    inner = jnp.sum(weights * grad_weights, axis=-1, keepdims=True)
    grad_scores = (weights * (grad_weights - inner)).astype(jnp.bfloat16)
    factor = HEAD_DIM ** (-0.5)
    grad_query = (
        jnp.einsum("shqk,skhe->sqhe", grad_scores, key_rows, preferred_element_type=jnp.float32)
        * factor
    )
    grad_key = (
        jnp.einsum("shqk,sqhe->skhe", grad_scores, query, preferred_element_type=jnp.float32)
        * factor
    )
    grad_value = jnp.einsum(
        "shqk,sqhe->skhe",
        weights.astype(jnp.bfloat16),
        grad_mixed,
        preferred_element_type=jnp.float32,
    )
    return (
        grad_query.astype(jnp.bfloat16),
        grad_key.astype(jnp.bfloat16),
        grad_value.astype(jnp.bfloat16),
    )


def column_sum(matrix):
    return jnp.sum(matrix, axis=0, dtype=jnp.float32)


def per_device(
    hidden_in,
    encoder_states,
    positions,
    self_qkv,
    self_out,
    cross_query,
    cross_kv,
    cross_out,
    up_weight,
    down_weight,
    norm_gains,
    bias_rows,
    up_bias,
    out_grad,
):
    local_width = hidden_in.shape[1]
    local_units = up_weight.shape[1]
    group_rows = SEQ_MB * LEN
    zeros_f = jnp.float32
    grad_qkv = jnp.zeros((D, 3, local_width), zeros_f)
    grad_out = jnp.zeros((local_width, D), zeros_f)
    grad_cq = jnp.zeros((D, local_width), zeros_f)
    grad_ckv = jnp.zeros((D, 2, local_width), zeros_f)
    grad_co = jnp.zeros((local_width, D), zeros_f)
    grad_up = jnp.zeros((D, local_units), zeros_f)
    grad_down = jnp.zeros((local_units, D), zeros_f)
    gain_terms = jnp.zeros((3, local_width), zeros_f)
    bias_terms = jnp.zeros((10, local_width), zeros_f)
    upbias_terms = jnp.zeros((local_units,), zeros_f)
    outputs = []
    hidden_grads = []
    encoder_grads = []
    for batch_index in range(MICRO):
        weights_now = (
            lax.all_gather(self_qkv, "dp", axis=0, tiled=True),
            lax.all_gather(self_out, "dp", axis=1, tiled=True),
            lax.all_gather(cross_query, "dp", axis=0, tiled=True),
            lax.all_gather(cross_kv, "dp", axis=0, tiled=True),
            lax.all_gather(cross_out, "dp", axis=1, tiled=True),
            lax.all_gather(up_weight, "dp", axis=0, tiled=True),
            lax.all_gather(down_weight, "dp", axis=1, tiled=True),
        )
        qkv_full, out_full, cq_full, ckv_full, co_full, up_full, down_full = weights_now
        self_columns, cross_columns, query_transposed = (
            lax.all_to_all(out_full, "tp", split_axis=1, concat_axis=0, tiled=True),
            lax.all_to_all(co_full, "tp", split_axis=1, concat_axis=0, tiled=True),
            lax.all_to_all(cq_full.T, "tp", split_axis=1, concat_axis=0, tiled=True),
        )
        lower = batch_index * group_rows
        first_seq = batch_index * SEQ_MB
        resid = hidden_in[lower : lower + group_rows].astype(jnp.float32)
        frames = encoder_states[first_seq : first_seq + SEQ_MB]
        order = positions[first_seq : first_seq + SEQ_MB]
        visible = order[:, None, :] <= order[:, :, None]
        normed_a, unit_a, inverse_a = norm_forward(resid, norm_gains[0], bias_rows[0])
        triple = jnp.einsum("td,dcf->tcf", normed_a, qkv_full, preferred_element_type=jnp.float32)
        query = to_heads((triple[:, 0] + bias_rows[3]).astype(jnp.bfloat16), SEQ_MB)
        keys = to_heads(triple[:, 1].astype(jnp.bfloat16), SEQ_MB)
        values = to_heads((triple[:, 2] + bias_rows[4]).astype(jnp.bfloat16), SEQ_MB)
        mixed, log_self = attend_forward(query, keys, values, visible)
        mixed_rows = mixed.reshape(group_rows, local_width)
        self_share = jnp.dot(
            spread_heads(mixed_rows), self_columns, preferred_element_type=jnp.float32
        )
        first = resid + self_share + bias_rows[5]
        normed_c, unit_c, inverse_c = norm_forward(first, norm_gains[1], bias_rows[1])
        cross_q = to_heads(
            (jnp.dot(normed_c, cq_full, preferred_element_type=jnp.float32) + bias_rows[6]).astype(
                jnp.bfloat16
            ),
            SEQ_MB,
        )
        paired = jnp.einsum("sfd,dcg->sfcg", frames, ckv_full, preferred_element_type=jnp.float32)
        cross_k = to_heads(paired[:, :, 0].astype(jnp.bfloat16), SEQ_MB)
        cross_v = to_heads((paired[:, :, 1] + bias_rows[7]).astype(jnp.bfloat16), SEQ_MB)
        cross_mixed, log_cross = attend_forward(cross_q, cross_k, cross_v, None)
        cross_rows = cross_mixed.reshape(group_rows, local_width)
        cross_share = jnp.dot(
            spread_heads(cross_rows), cross_columns, preferred_element_type=jnp.float32
        )
        second = first + cross_share + bias_rows[8]
        normed_m, unit_m, inverse_m = norm_forward(second, norm_gains[2], bias_rows[2])
        before = jnp.dot(normed_m, up_full, preferred_element_type=jnp.float32) + up_bias
        activated = jax.nn.gelu(before, approximate=False).astype(jnp.bfloat16)
        final = (
            second
            + branch_total(jnp.dot(activated, down_full, preferred_element_type=jnp.float32))
            + bias_rows[9]
        )
        outputs.append(final.astype(jnp.bfloat16))
        weights_back = (
            lax.all_gather(self_qkv, "dp", axis=0, tiled=True),
            lax.all_gather(self_out, "dp", axis=1, tiled=True),
            lax.all_gather(cross_query, "dp", axis=0, tiled=True),
            lax.all_gather(cross_kv, "dp", axis=0, tiled=True),
            lax.all_gather(cross_out, "dp", axis=1, tiled=True),
            lax.all_gather(up_weight, "dp", axis=0, tiled=True),
            lax.all_gather(down_weight, "dp", axis=1, tiled=True),
        )
        qkv_back, out_back, cq_back, ckv_back, co_back, up_back, down_back = weights_back
        grad_final = out_grad[lower : lower + group_rows]
        grad_final_full = spread_grad(grad_final)
        grad_down = grad_down + jnp.einsum(
            "tf,td->fd", activated, grad_final_full, preferred_element_type=jnp.float32
        )
        grad_act = jnp.einsum(
            "td,fd->tf", grad_final_full, down_back, preferred_element_type=jnp.float32
        )
        normal_cdf = 0.5 * (1.0 + lax.erf(before / math.sqrt(2.0)))
        density = jnp.exp(-0.5 * before * before) / math.sqrt(2.0 * math.pi)
        grad_before = (grad_act * (normal_cdf + before * density)).astype(jnp.bfloat16)
        grad_up = grad_up + jnp.einsum(
            "td,tf->df", normed_m, grad_before, preferred_element_type=jnp.float32
        )
        grad_norm_m = input_total(
            jnp.einsum("tf,df->td", grad_before, up_back, preferred_element_type=jnp.float32)
        )
        back_m, gain_m, shift_m = norm_backward(grad_norm_m, unit_m, inverse_m, norm_gains[2])
        grad_second = grad_final.astype(jnp.float32) + back_m
        grad_cross_full = spread_grad(grad_second)
        grad_co = grad_co + jnp.einsum(
            "tg,td->gd", cross_rows, grad_cross_full, preferred_element_type=jnp.float32
        )
        grad_cross_mixed = to_heads(
            jnp.einsum(
                "td,gd->tg", grad_cross_full, co_back, preferred_element_type=jnp.float32
            ).astype(jnp.bfloat16),
            SEQ_MB,
        )
        grad_cq_heads, grad_ck_heads, grad_cv_heads = attend_backward(
            cross_q, cross_k, cross_v, None, log_cross, grad_cross_mixed
        )
        grad_cq_rows = grad_cq_heads.reshape(group_rows, local_width)
        grad_kv = jnp.stack(
            [
                grad_ck_heads.reshape(SEQ_MB, -1, local_width),
                grad_cv_heads.reshape(SEQ_MB, -1, local_width),
            ],
            axis=2,
        )
        grad_cq = grad_cq + jnp.einsum(
            "td,tg->dg", normed_c, grad_cq_rows, preferred_element_type=jnp.float32
        )
        grad_ckv = grad_ckv + jnp.einsum(
            "sfd,sfcg->dcg", frames, grad_kv, preferred_element_type=jnp.float32
        )
        frame_partial = jnp.einsum(
            "sfcg,dcg->sfd", grad_kv, ckv_back, preferred_element_type=jnp.float32
        )
        encoder_grads.append(
            lax.psum_scatter(
                frame_partial.astype(jnp.bfloat16), "tp", scatter_dimension=2, tiled=True
            ).astype(jnp.float32)
        )
        grad_norm_c = jnp.dot(
            spread_heads(grad_cq_rows), query_transposed, preferred_element_type=jnp.float32
        )
        back_c, gain_c, shift_c = norm_backward(grad_norm_c, unit_c, inverse_c, norm_gains[1])
        grad_first = grad_second + back_c
        grad_self_full = spread_grad(grad_first)
        grad_out = grad_out + jnp.einsum(
            "tg,td->gd", mixed_rows, grad_self_full, preferred_element_type=jnp.float32
        )
        grad_mixed = to_heads(
            jnp.einsum(
                "td,gd->tg", grad_self_full, out_back, preferred_element_type=jnp.float32
            ).astype(jnp.bfloat16),
            SEQ_MB,
        )
        grad_q_heads, grad_k_heads, grad_v_heads = attend_backward(
            query, keys, values, visible, log_self, grad_mixed
        )
        grad_triple = jnp.stack(
            [
                grad_q_heads.reshape(group_rows, local_width),
                grad_k_heads.reshape(group_rows, local_width),
                grad_v_heads.reshape(group_rows, local_width),
            ],
            axis=1,
        )
        grad_qkv = grad_qkv + jnp.einsum(
            "td,tcg->dcg", normed_a, grad_triple, preferred_element_type=jnp.float32
        )
        grad_norm_a = input_total(
            jnp.einsum("tcg,dcg->td", grad_triple, qkv_back, preferred_element_type=jnp.float32)
        )
        back_a, gain_a, shift_a = norm_backward(grad_norm_a, unit_a, inverse_a, norm_gains[0])
        hidden_grads.append(grad_first + back_a)
        gain_terms = gain_terms + jnp.stack([gain_a, gain_c, gain_m])
        bias_terms = bias_terms + jnp.stack(
            [
                shift_a,
                shift_c,
                shift_m,
                column_sum(grad_triple[:, 0]),
                column_sum(grad_triple[:, 2]),
                column_sum(grad_first.astype(jnp.bfloat16)),
                column_sum(grad_cq_rows),
                column_sum(grad_kv[:, :, 1].reshape(-1, local_width)),
                column_sum(grad_second.astype(jnp.bfloat16)),
                column_sum(grad_final),
            ]
        )
        upbias_terms = upbias_terms + column_sum(grad_before)
    weight_totals = (
        lax.psum_scatter(
            grad_qkv.astype(jnp.bfloat16), "dp", scatter_dimension=0, tiled=True
        ).astype(jnp.float32),
        lax.psum_scatter(
            grad_out.astype(jnp.bfloat16), "dp", scatter_dimension=1, tiled=True
        ).astype(jnp.float32),
        lax.psum_scatter(
            grad_cq.astype(jnp.bfloat16), "dp", scatter_dimension=0, tiled=True
        ).astype(jnp.float32),
        lax.psum_scatter(
            grad_ckv.astype(jnp.bfloat16), "dp", scatter_dimension=0, tiled=True
        ).astype(jnp.float32),
        lax.psum_scatter(
            grad_co.astype(jnp.bfloat16), "dp", scatter_dimension=1, tiled=True
        ).astype(jnp.float32),
        lax.psum_scatter(
            grad_up.astype(jnp.bfloat16), "dp", scatter_dimension=0, tiled=True
        ).astype(jnp.float32),
        lax.psum_scatter(
            grad_down.astype(jnp.bfloat16), "dp", scatter_dimension=1, tiled=True
        ).astype(jnp.float32),
    )
    vector_totals = lax.psum((gain_terms, bias_terms, upbias_terms), "dp")
    return (
        jnp.concatenate(outputs, axis=0),
        jnp.concatenate(hidden_grads, axis=0),
        jnp.concatenate(encoder_grads, axis=0),
        weight_totals[0],
        weight_totals[1],
        weight_totals[2],
        weight_totals[3],
        weight_totals[4],
        weight_totals[5],
        weight_totals[6],
        vector_totals[0],
        vector_totals[1],
        vector_totals[2],
    )


def solution(mesh):
    in_specs = (
        P("dp", "tp"),
        P("dp", None, None),
        P("dp", None),
        P("dp", None, "tp"),
        P("tp", "dp"),
        P("dp", "tp"),
        P("dp", None, "tp"),
        P("tp", "dp"),
        P("dp", "tp"),
        P("tp", "dp"),
        P(None, "tp"),
        P(None, "tp"),
        P("tp"),
        P("dp", "tp"),
    )
    out_specs = (
        P("dp", "tp"),
        P("dp", "tp"),
        P("dp", None, "tp"),
        P("dp", None, "tp"),
        P("tp", "dp"),
        P("dp", "tp"),
        P("dp", None, "tp"),
        P("tp", "dp"),
        P("dp", "tp"),
        P("tp", "dp"),
        P(None, "tp"),
        P(None, "tp"),
        P("tp"),
    )
    columns, shards = mesh.shape["tp"], mesh.shape["dp"]
    powers = columns & (columns - 1) == 0 and shards & (shards - 1) == 0

    def device_step(*arrays):
        seqs = arrays[2].shape[0]
        wide = arrays[0].shape[1] % LANES == 0
        if powers and wide and columns == 2 and seqs % columns == 0 and shards >= 8:
            return per_device_whole_sequences(*arrays)
        return per_device(*arrays)

    return jax.shard_map(
        device_step, mesh=mesh, in_specs=in_specs, out_specs=out_specs, check_vma=False
    )
```
